32 devices in a mesh: dp: 2 (over core), expert: 8 (over z, y), tensor: 2 (over x).
Axes of the slice: x: 2, y: 2, z: 4, core: 2. Of those that a mesh axis runs over, the one named last changes fastest.
Arguments:
- tokens: bfloat16 [3152, 768], P(('dp', 'expert')), may hold values from -41 to 41, as said below
- ln1_scale: float32 [768], replicated, may hold values from 0.25 to 1.75
- ln1_bias: float32 [768], replicated, may hold values from -3 to 3
- w_qkv: bfloat16 [768, 3, 768], P(None, None, 'tensor'), may hold values from -0.21875 to 0.21875
- w_out: bfloat16 [768, 768], P('tensor'), may hold values from -0.875 to 0.875
- b_out: float32 [768], replicated, may hold values from -3 to 3
- ln2_scale: float32 [768], replicated, may hold values from 0.25 to 1.75
- ln2_bias: float32 [768], replicated, may hold values from -3 to 3
- w_router: bfloat16 [768, 8], replicated, may hold values from -0.09375 to 0.09375
- w_in: bfloat16 [8, 768, 3072], P('expert', None, 'tensor'), may hold values from -0.21875 to 0.21875
- b_in: float32 [8, 3072], P('expert', 'tensor'), may hold values from -3 to 3
- w_exp_out: bfloat16 [8, 3072, 768], P('expert', 'tensor'), may hold values from -1.75 to 1.75
- b_exp_out: float32 [8, 768], P('expert'), may hold values from -12 to 12
- routes: int32 [3152, 2], P(('dp', 'expert')), may hold values from 0 to 7, all different within a row
- cotangent: bfloat16 [3152, 768], P(('dp', 'expert')), may hold values from -6 to 6
Outputs:
- out: bfloat16 [3152, 768], P(('dp', 'expert'))
- grad_tokens: bfloat16 [3152, 768], P(('dp', 'expert'))
- grad_ln1_scale: float32 [768], P(('dp', 'expert'))
- grad_ln1_bias: float32 [768], P(('dp', 'expert'))
- grad_w_qkv: float32 [768, 3, 768], P(('dp', 'expert'), None, 'tensor')
- grad_w_out: float32 [768, 768], P('tensor', ('dp', 'expert'))
- grad_b_out: float32 [768], P(('dp', 'expert'))
- grad_ln2_scale: float32 [768], P(('dp', 'expert'))
- grad_ln2_bias: float32 [768], P(('dp', 'expert'))
- grad_router: float32 [768, 8], P(('dp', 'expert'))
- grad_w_in: float32 [8, 768, 3072], P('expert', None, 'tensor')
- grad_b_in: float32 [8, 3072], P('expert', 'tensor')
- grad_w_exp_out: float32 [8, 3072, 768], P('expert', 'tensor')
- grad_b_exp_out: float32 [8, 768], P('expert')
The draws below stay inside these ranges and needn't reach their ends.
Inputs may be any that keep to these rules, and one draw needn't show every extreme that they name: `routes`: each token names two different experts, and every expert is named by some token. `tokens`: real values of varied scale.
All inputs are finite; a program needn't handle non-finite values.
Results may differ from the reference program's by a relative error of at most 0.014.
Values may be sent and summed in bfloat16 or wider, within the bound.
No kernel may reach another device: no remote copies, remote signals or barrier semaphores. Data moves between devices by JAX's collectives and lax.ppermute only.
A program may use at most 128 MiB of HBM per device.

```python
import math
import jax
import jax.numpy as jnp
from jax import lax

D = 768
HEADS = 12
HEAD_DIM = 64
FF = 3072
LEN = 197
SEQ_DEV = 1
E = 8
HHD = 768
TOK_DEV = 197
TOKENS = 3152
CAP = 62
N_DP = 2
N_EXPERT = 8


def draw_tokens(key, part):
    key_base, key_rows, key_cols = jax.random.split(key, 3)
    row_scale = 0.5 * jnp.exp(jax.random.uniform(key_rows, (TOKENS, 1), jnp.float32, 0.0, math.log(10.0)))
    col_scale = 0.5 * jnp.exp(jax.random.uniform(key_cols, (1, D), jnp.float32, 0.0, math.log(4.0)))
    base = jnp.clip(jax.random.normal(key_base, (TOKENS, D), jnp.float32), -4.0, 4.0)
    return (base * row_scale * col_scale).astype(jnp.bfloat16)


def level_of(stream_key, extent, pieces, smallest, largest):
    level, own = 1.0, jax.random.fold_in(stream_key, 6)
    for dim, blocks in pieces:
        heights = jnp.exp(jax.random.uniform(jax.random.fold_in(own, dim), (blocks,), jnp.float32, smallest / len(pieces), largest / len(pieces)))
        level = level * jnp.repeat(heights, extent[dim] // blocks).reshape([-1 if axis == dim else 1 for axis in range(len(extent))])
    return level


def different_ones(key, rows, count, top, lift):
    ranking = jax.random.permutation(jax.random.fold_in(key, 1), count)
    boost = ranking
    for power in range(3):
        boost = boost * boost // count
    boost = boost * lift // count
    tickets = jax.random.randint(jax.random.fold_in(key, 2), (rows, count), 0, 4096) + boost
    sure = jax.random.permutation(jax.random.fold_in(key, 3), rows)[jnp.arange(count) % rows]
    tickets = jnp.where(jnp.arange(rows)[:, None] == sure[None, :], 1 << 14, tickets)
    merit = tickets * count + jnp.arange(count)
    return lax.top_k(merit.astype(jnp.int32), top)[1].astype(jnp.int32)


def scatter_about(stream_key, dims, spread, reach, pieces=(), held_as=jnp.bfloat16):
    loudness = level_of(stream_key, dims, pieces, -0.22, 0.18) if pieces else 1.0
    drawn = jax.random.normal(stream_key, dims, jnp.float32) * spread * loudness
    return jnp.minimum(jnp.maximum(drawn, -reach), reach).astype(held_as)


def setup_inputs(seed: int = 0) -> dict:
    seeds = jax.random.split(jax.random.key(seed), 16)
    return {
        "tokens": draw_tokens(jax.random.fold_in(seeds[15], 71), 0),
        "ln1_scale": jnp.clip(1.0 + 0.15 * jax.random.normal(seeds[1], (D,), jnp.float32), 0.25, 1.75),
        "ln1_bias": scatter_about(seeds[2], (D,), 0.5, 3.0, (), jnp.float32),
        "w_qkv": scatter_about(seeds[3], (D, 3, HHD), D ** -0.5, 0.21875, ((2, 2),)),
        "w_out": scatter_about(seeds[4], (HHD, D), (HHD // 16) ** -0.5, 0.875, ((0, 2),)),
        "b_out": scatter_about(seeds[5], (D,), 0.5, 3.0, (), jnp.float32),
        "ln2_scale": jnp.clip(1.0 + 0.15 * jax.random.normal(seeds[6], (D,), jnp.float32), 0.25, 1.75),
        "ln2_bias": scatter_about(seeds[7], (D,), 0.5, 3.0, (), jnp.float32),
        "w_router": scatter_about(seeds[8], (D, E), (5 * D) ** -0.5, 0.09375),
        "w_in": scatter_about(seeds[9], (E, D, FF), D ** -0.5, 0.21875, ((0, 8), (2, 2))),
        "b_in": scatter_about(seeds[10], (E, FF), 0.5, 3.0, ((0, 8), (1, 2)), jnp.float32),
        "w_exp_out": scatter_about(seeds[11], (E, FF, D), (max(FF // 256, 1)) ** -0.5, 1.75, ((0, 8), (1, 2))),
        "b_exp_out": scatter_about(seeds[12], (E, D), 2.0, 12.0, ((0, 8),), jnp.float32),
        "routes": different_ones(seeds[13], TOKENS, E, 2, 2048),
        "cotangent": scatter_about(seeds[14], (TOKENS, D), 1.0, 6.0, ((0, 16),)),
    }


EPSILON = 1e-06

def rounded(values):
    return lax.optimization_barrier(values.astype(jnp.bfloat16))

def layer_norm(values, scale, shift):
    mean_val = lax.optimization_barrier(jnp.mean(values, axis=-1, keepdims=True))
    centred = values - mean_val
    inv_std = lax.rsqrt(lax.optimization_barrier(jnp.mean(centred * centred, axis=-1, keepdims=True)) + EPSILON)
    x_hat = centred * inv_std
    return (x_hat * scale + shift, x_hat, inv_std)

def norm_back(grad, x_hat, inv_std, scale):
    scaled = grad * scale
    return inv_std * (scaled - lax.optimization_barrier(jnp.mean(scaled, axis=-1, keepdims=True)) - x_hat * lax.optimization_barrier(jnp.mean(scaled * x_hat, axis=-1, keepdims=True)))

def route_slots(route_rows, expert_count, capacity):
    chosen = jnp.concatenate([route_rows[:, 0], route_rows[:, 1]]).astype(jnp.int32)
    one_hot = (chosen[:, None] == jnp.arange(expert_count, dtype=jnp.int32)[None, :]).astype(jnp.int32)
    earlier = jnp.cumsum(one_hot, axis=0, dtype=jnp.int32) - one_hot
    slot_index = lax.optimization_barrier(jnp.sum(earlier * one_hot, axis=1, dtype=jnp.int32))
    kept_mask = slot_index < capacity
    target = jnp.where(kept_mask, chosen * capacity + slot_index, expert_count * capacity).astype(jnp.int32)
    return (one_hot, kept_mask, target)

def split_heads(qkv_rows, seq_count, head_count):
    shape_heads = (seq_count, LEN, head_count, HEAD_DIM)
    query = qkv_rows[0].astype(jnp.float32).reshape(shape_heads)
    keys = qkv_rows[1].astype(jnp.float32).reshape(shape_heads)
    values = qkv_rows[2].astype(jnp.float32).reshape(shape_heads)
    return (query, keys, values)

def attend(qkv_rows, seq_count, head_count):
    query, keys, values = split_heads(qkv_rows, seq_count, head_count)
    scores = jnp.einsum('sqhe,skhe->shqk', query, keys) * HEAD_DIM ** (-0.5)
    log_sum = jnp.log(lax.optimization_barrier(jnp.sum(jnp.exp(scores), axis=-1)))
    weights = rounded(jnp.exp(scores - log_sum[..., None])).astype(jnp.float32)
    attended = jnp.einsum('shqk,skhe->sqhe', weights, values).astype(jnp.bfloat16)
    return (attended.reshape(seq_count * LEN, head_count * HEAD_DIM), log_sum)

def attend_back(qkv_rows, log_sum, grad_attended, seq_count, head_count):
    query, keys, values = split_heads(qkv_rows, seq_count, head_count)
    scaling = HEAD_DIM ** (-0.5)
    scores = jnp.einsum('sqhe,skhe->shqk', query, keys) * scaling
    weights32 = jnp.exp(scores - log_sum[..., None])
    weights_r = rounded(weights32).astype(jnp.float32)
    grad_out = grad_attended.astype(jnp.float32).reshape(seq_count, LEN, head_count, HEAD_DIM)
    grad_values = jnp.einsum('shqk,sqhe->skhe', weights_r, grad_out).astype(jnp.bfloat16)
    grad_weights = jnp.einsum('sqhe,skhe->shqk', grad_out, values)
    delta = lax.optimization_barrier(jnp.sum(weights32 * grad_weights, axis=-1, keepdims=True))
    grad_scores = rounded(weights32 * (grad_weights - delta) * scaling).astype(jnp.float32)
    grad_query = jnp.einsum('shqk,skhe->sqhe', grad_scores, keys).astype(jnp.bfloat16)
    grad_keys = jnp.einsum('shqk,sqhe->skhe', grad_scores, query).astype(jnp.bfloat16)
    stacked = jnp.stack([grad_query, grad_keys, grad_values])
    return stacked.reshape(3, seq_count * LEN, head_count * HEAD_DIM)

def reference(tokens, ln1_scale, ln1_bias, w_qkv, w_out, b_out, ln2_scale, ln2_bias, w_router, w_in, b_in, w_exp_out, b_exp_out, routes, cotangent):
    groups = N_DP * N_EXPERT
    slot_total = E * CAP
    tok_blocks = tokens.reshape(groups, TOK_DEV, D)
    route_blocks = routes.reshape(groups, TOK_DEV, 2)
    grad_blocks = cotangent.reshape(groups, TOK_DEV, D)
    w_qkv_f = w_qkv.astype(jnp.float32)

    def forward_block(inputs):
        block, route_rows = inputs
        block_f = block.astype(jnp.float32)
        normed1, x_hat1, inv_std1 = layer_norm(block_f, ln1_scale, ln1_bias)
        normed1_b = rounded(normed1)
        qkv_rows = jnp.einsum('td,dch->cth', normed1_b.astype(jnp.float32), w_qkv_f).astype(jnp.bfloat16)
        attended, log_sum = attend(qkv_rows, SEQ_DEV, HEADS)
        mixed = block_f + jnp.dot(attended, w_out, preferred_element_type=jnp.float32) + b_out
        normed2, x_hat2, inv_std2 = layer_norm(mixed, ln2_scale, ln2_bias)
        normed2_b = normed2.astype(jnp.bfloat16)
        logits = jnp.dot(normed2_b, w_router, preferred_element_type=jnp.float32)
        exp_logits = jnp.exp(logits)
        router_probs = exp_logits / lax.optimization_barrier(jnp.sum(exp_logits, axis=-1, keepdims=True))
        one_hot, kept_mask, target = route_slots(route_rows, E, CAP)
        both_rows = jnp.concatenate([normed2_b, normed2_b])
        buffer = jnp.zeros((slot_total, D), jnp.bfloat16).at[target].set(both_rows, mode='drop')
        return (normed1_b, qkv_rows, log_sum, attended, mixed, x_hat1, inv_std1, x_hat2, inv_std2, normed2_b, router_probs, one_hot, kept_mask, target, buffer)
    saved = lax.map(forward_block, (tok_blocks, route_blocks))
    normed1_all, qkv_all, lse_all, attended_all, mixed_all, x_hat1_all, inv1_all, x_hat2_all, inv2_all, normed2_all, probs_all, onehot_all, kept_all, target_all, buffer_all = saved
    expert_rows = buffer_all.reshape(groups, E, CAP, D).transpose(1, 0, 2, 3).reshape(E, groups * CAP, D)

    def expert_forward(inputs):
        rows, first, first_bias, second, second_bias = inputs
        pre_act = jnp.dot(rows, first, preferred_element_type=jnp.float32) + first_bias
        hidden = jax.nn.gelu(pre_act).astype(jnp.bfloat16)
        return (jnp.dot(hidden, second, preferred_element_type=jnp.float32) + second_bias).astype(jnp.bfloat16)
    expert_result = lax.map(expert_forward, (expert_rows, w_in, b_in, w_exp_out, b_exp_out))
    token_side = expert_result.reshape(E, groups, CAP, D).transpose(1, 0, 2, 3).reshape(groups, slot_total, D)

    def combine_block(inputs):
        mixed, router_probs, route_rows, kept_mask, target, output_rows, grad_rows = inputs
        chosen_probs = jnp.take_along_axis(router_probs, route_rows, axis=1)
        gate_flat = jnp.concatenate([chosen_probs[:, 0], chosen_probs[:, 1]])
        gate_kept = jnp.where(kept_mask, gate_flat, jnp.float32(0.0))
        picked = jnp.take(output_rows, jnp.minimum(target, slot_total - 1), axis=0).astype(jnp.float32)
        weighted = gate_kept[:, None] * picked
        result = (mixed + weighted[:TOK_DEV] + weighted[TOK_DEV:]).astype(jnp.bfloat16)
        grad_f = grad_rows.astype(jnp.float32)
        grad_twice = jnp.concatenate([grad_f, grad_f])
        gate_grad = jnp.where(kept_mask, lax.optimization_barrier(jnp.sum(grad_twice * picked, axis=1)), jnp.float32(0.0))
        grad_sent = (gate_kept[:, None] * grad_twice).astype(jnp.bfloat16)
        grad_buffer = jnp.zeros((slot_total, D), jnp.bfloat16).at[target].set(grad_sent, mode='drop')
        return (result, gate_grad, grad_buffer)
    result_all, gate_grad_all, grad_buffer_all = lax.map(combine_block, (mixed_all, probs_all, route_blocks, kept_all, target_all, token_side, grad_blocks))
    grad_expert_rows = grad_buffer_all.reshape(groups, E, CAP, D).transpose(1, 0, 2, 3).reshape(E, groups * CAP, D)

    def expert_backward(inputs):
        rows, grad_out_rows, first, first_bias, second = inputs
        pre_act = jnp.dot(rows, first, preferred_element_type=jnp.float32) + first_bias
        hidden = jax.nn.gelu(pre_act).astype(jnp.bfloat16)
        grad_second = jnp.dot(hidden.T, grad_out_rows, preferred_element_type=jnp.float32)
        grad_second_bias = lax.optimization_barrier(jnp.sum(grad_out_rows.astype(jnp.float32), axis=0))
        grad_hidden = jnp.dot(grad_out_rows, second.T, preferred_element_type=jnp.float32)
        grad_pre = jax.vjp(jax.nn.gelu, pre_act)[1](grad_hidden)[0].astype(jnp.bfloat16)
        grad_first = jnp.dot(rows.T, grad_pre, preferred_element_type=jnp.float32)
        grad_first_bias = lax.optimization_barrier(jnp.sum(grad_pre.astype(jnp.float32), axis=0))
        grad_rows = jnp.dot(grad_pre, first.T, preferred_element_type=jnp.float32).astype(jnp.bfloat16)
        return (grad_first, grad_first_bias, grad_second, grad_second_bias, grad_rows)
    grad_w_in, grad_b_in, grad_w_exp_out, grad_b_exp_out, grad_rows_all = lax.map(expert_backward, (expert_rows, grad_expert_rows, w_in, b_in, w_exp_out))
    grad_rows_tok = grad_rows_all.reshape(E, groups, CAP, D).transpose(1, 0, 2, 3).reshape(groups, slot_total, D)

    def backward_block(carry, inputs):
        normed1_b, qkv_rows, log_sum, attended, x_hat1, inv1, x_hat2, inv2, normed2_b, router_probs, one_hot, kept_mask, target, gate_grad, grad_rows_b, grad_block = inputs
        grad_f = grad_block.astype(jnp.float32)
        picked = jnp.take(grad_rows_b, jnp.minimum(target, slot_total - 1), axis=0).astype(jnp.float32)
        picked = jnp.where(kept_mask[:, None], picked, jnp.float32(0.0))
        one_hot_f = one_hot.astype(jnp.float32)
        grad_probs = one_hot_f[:TOK_DEV] * gate_grad[:TOK_DEV, None] + one_hot_f[TOK_DEV:] * gate_grad[TOK_DEV:, None]
        grad_logits = (router_probs * (grad_probs - lax.optimization_barrier(jnp.sum(router_probs * grad_probs, axis=1, keepdims=True)))).astype(jnp.bfloat16)
        grad_normed2 = picked[:TOK_DEV] + picked[TOK_DEV:] + jnp.dot(grad_logits, w_router.T, preferred_element_type=jnp.float32)
        grad_router = jnp.dot(normed2_b.T, grad_logits, preferred_element_type=jnp.float32)
        grad_ln2_scale = lax.optimization_barrier(jnp.sum(grad_normed2 * x_hat2, axis=0))
        grad_ln2_bias = lax.optimization_barrier(jnp.sum(grad_normed2, axis=0))
        grad_mixed = grad_f + norm_back(grad_normed2, x_hat2, inv2, ln2_scale)
        grad_b_out = lax.optimization_barrier(jnp.sum(grad_mixed, axis=0))
        grad_mixed_b = grad_mixed.astype(jnp.bfloat16)
        grad_w_out = jnp.dot(attended.T, grad_mixed_b, preferred_element_type=jnp.float32)
        grad_attended = jnp.dot(grad_mixed_b, w_out.T, preferred_element_type=jnp.float32).astype(jnp.bfloat16)
        grad_qkv = attend_back(qkv_rows, log_sum, grad_attended, SEQ_DEV, HEADS)
        grad_qkv_f = grad_qkv.astype(jnp.float32)
        grad_w_qkv = jnp.einsum('td,cth->dch', normed1_b.astype(jnp.float32), grad_qkv_f)
        grad_normed1 = jnp.einsum('cth,dch->td', grad_qkv_f, w_qkv_f)
        grad_ln1_scale = lax.optimization_barrier(jnp.sum(grad_normed1 * x_hat1, axis=0))
        grad_ln1_bias = lax.optimization_barrier(jnp.sum(grad_normed1, axis=0))
        grad_tok = (grad_mixed + norm_back(grad_normed1, x_hat1, inv1, ln1_scale)).astype(jnp.bfloat16)
        terms = (grad_ln1_scale, grad_ln1_bias, grad_w_qkv, grad_w_out, grad_b_out, grad_ln2_scale, grad_ln2_bias, grad_router)
        carry = tuple((total + term for total, term in zip(carry, terms)))
        return (carry, grad_tok)
    init = (jnp.zeros((D,), jnp.float32), jnp.zeros((D,), jnp.float32), jnp.zeros((D, 3, HHD), jnp.float32), jnp.zeros((HHD, D), jnp.float32), jnp.zeros((D,), jnp.float32), jnp.zeros((D,), jnp.float32), jnp.zeros((D,), jnp.float32), jnp.zeros((D, E), jnp.float32))
    sums, grad_tok_all = lax.scan(backward_block, init, (normed1_all, qkv_all, lse_all, attended_all, x_hat1_all, inv1_all, x_hat2_all, inv2_all, normed2_all, probs_all, onehot_all, kept_all, target_all, gate_grad_all, grad_rows_tok, grad_blocks))
    return (result_all.reshape(TOKENS, D), grad_tok_all.reshape(TOKENS, D), sums[0], sums[1], sums[2], sums[3], sums[4], sums[5], sums[6], sums[7], grad_w_in, grad_b_in, grad_w_exp_out, grad_b_exp_out)
```

```python
import jax
import jax.numpy as jnp
from jax import lax
from jax.sharding import PartitionSpec as P

HEAD_DIM = 64
LEN = 197
EPSILON = 1e-06
BF = jnp.bfloat16
F32 = jnp.float32


def layer_norm(values, scale, shift):
    mean_val = jnp.mean(values, axis=-1, keepdims=True)
    centred = values - mean_val
    inv_std = lax.rsqrt(jnp.mean(centred * centred, axis=-1, keepdims=True) + EPSILON)
    x_hat = centred * inv_std
    return (x_hat * scale + shift, x_hat, inv_std)


def norm_back(grad, x_hat, inv_std, scale):
    scaled = grad * scale
    return inv_std * (
        scaled
        - jnp.mean(scaled, axis=-1, keepdims=True)
        - x_hat * jnp.mean(scaled * x_hat, axis=-1, keepdims=True)
    )


def dot32(a, b):
    return jnp.dot(a, b, preferred_element_type=F32)


def swap(x, axis):
    return lax.ppermute(x, axis, [(0, 1), (1, 0)])


def xor_all_to_all(blocks):
    count = blocks.shape[0]
    outs = [blocks[0]]
    for k in range(1, count):
        outs.append(lax.ppermute(blocks[k], "expert", [(i, i ^ k) for i in range(count)]))
    return outs


def halve(parts, axis_name, bit, index):
    size = lax.axis_size(axis_name)
    own_bit = (index // bit) % 2
    sent = lax.dynamic_index_in_dim(parts, 1 - own_bit, 0, keepdims=False)
    kept = lax.dynamic_index_in_dim(parts, own_bit, 0, keepdims=False)
    got = lax.ppermute(sent, axis_name, [(i, i ^ bit) for i in range(size)])
    return kept.astype(F32) + got.astype(F32)


def reduce_dense(partial):
    count = lax.axis_size("expert")
    me = lax.axis_index("expert")
    rows = partial.shape[0] // (2 * count)
    cols = partial.shape[1]
    part = partial.astype(BF).reshape(2, count * rows, cols)
    part = halve(part, "dp", 1, lax.axis_index("dp"))
    bit = 1
    left = count
    while left > 1:
        part = part.astype(BF).reshape(left // 2, 2, rows, cols).swapaxes(0, 1)
        part = halve(part, "expert", bit, me)
        bit *= 2
        left //= 2
    return part.reshape(rows, cols)


def reduce_small(blocks):
    count = blocks.shape[0]
    me = lax.axis_index("dp") * lax.axis_size("expert") + lax.axis_index("expert")
    total = lax.dynamic_index_in_dim(blocks, me, 0, keepdims=False)
    for k in range(1, count):
        piece = lax.dynamic_index_in_dim(blocks, me ^ k, 0, keepdims=False)
        total = total + lax.ppermute(
            piece, ("dp", "expert"), [(i, i ^ k) for i in range(count)]
        )
    return total


def gelu_both(u):
    c0 = 0.7978845608028654
    inner = c0 * (u + 0.044715 * u * u * u)
    th = jnp.tanh(inner)
    value = 0.5 * u * (1.0 + th)
    slope = 0.5 * (1.0 + th) + 0.5 * u * (1.0 - th * th) * c0 * (1.0 + 3.0 * 0.044715 * u * u)
    return value, slope


def per_device(
    tokens,
    ln1_scale,
    ln1_bias,
    w_qkv,
    w_out,
    b_out,
    ln2_scale,
    ln2_bias,
    w_router,
    w_in,
    b_in,
    w_exp_out,
    b_exp_out,
    routes,
    cotangent,
):
    row_count, width = tokens.shape
    expert_count = w_router.shape[1]
    group_count = lax.axis_size("expert")
    me = lax.axis_index("expert")
    tensor_id = lax.axis_index("tensor")
    capacity = (5 * row_count + 2 * expert_count - 1) // (2 * expert_count)
    cap_pad = -(-(capacity + 1) // 16) * 16
    slot_total = expert_count * cap_pad
    seq_count = row_count // LEN
    head_count = w_qkv.shape[2] // HEAD_DIM
    hidden_width = head_count * HEAD_DIM
    shape_heads = (seq_count, LEN, head_count, HEAD_DIM)
    scaling = HEAD_DIM ** (-0.5)
    w_in = w_in[0]
    w_exp_out = w_exp_out[0]
    w_out_other = swap(w_out, "tensor")
    chosen = jnp.concatenate([routes[:, 0], routes[:, 1]])
    one_hot = (chosen[:, None] == jnp.arange(expert_count, dtype=jnp.int32)[None, :]).astype(BF)
    entry = jnp.arange(2 * row_count, dtype=jnp.int32)
    before = (entry[:, None] > entry[None, :]).astype(BF)
    earlier = dot32(before, one_hot)
    slot_index = jnp.sum(earlier * one_hot.astype(F32), axis=1).astype(jnp.int32)
    kept = slot_index < capacity
    target = jnp.where(kept, (chosen ^ me) * cap_pad + slot_index, slot_total)
    slot_ids = jnp.arange(slot_total, dtype=jnp.int32)
    place0 = slot_ids[:, None] == target[None, :row_count]
    place1 = slot_ids[:, None] == target[None, row_count:]
    placing = (place0 | place1).astype(BF)
    cot_buffer = dot32(placing, cotangent).astype(BF).reshape(expert_count, cap_pad, width)
    cot_rows = jnp.concatenate(xor_all_to_all(cot_buffer))
    tok_float = tokens.astype(F32)
    normed1, x_hat1, inv_std1 = layer_norm(tok_float, ln1_scale, ln1_bias)
    normed1_b = normed1.astype(BF)
    qkv_rows = jnp.einsum("td,dch->cth", normed1_b, w_qkv, preferred_element_type=F32).astype(BF)
    query = qkv_rows[0].reshape(shape_heads)
    key_rows = qkv_rows[1].reshape(shape_heads)
    value_rows = qkv_rows[2].reshape(shape_heads)
    scores = jnp.einsum("sqhe,skhe->shqk", query, key_rows, preferred_element_type=F32) * scaling
    log_sum = jnp.log(jnp.sum(jnp.exp(scores), axis=-1, keepdims=True))
    weights_b = jnp.exp(scores - log_sum).astype(BF)
    attended = jnp.einsum(
        "shqk,skhe->sqhe", weights_b, value_rows, preferred_element_type=F32
    ).astype(BF)
    attended = attended.reshape(row_count, hidden_width)
    attended_other = swap(attended, "tensor")
    raw_hidden = lax.dot_general(
        cot_rows, w_exp_out, (((1,), (1,)), ((), ())), preferred_element_type=F32
    )
    mixed = tok_float + (dot32(attended, w_out) + dot32(attended_other, w_out_other)) + b_out
    normed2, x_hat2, inv_std2 = layer_norm(mixed, ln2_scale, ln2_bias)
    normed2_b = normed2.astype(BF)
    logits = dot32(normed2_b, w_router)
    exp_logits = jnp.exp(logits)
    router_probs = exp_logits / jnp.sum(exp_logits, axis=-1, keepdims=True)
    one_hot_f = one_hot.astype(F32)
    gate0 = jnp.sum(router_probs * one_hot_f[:row_count], axis=1)
    gate1 = jnp.sum(router_probs * one_hot_f[row_count:], axis=1)
    gate_slot = jnp.sum(
        jnp.where(place0, gate0[None, :], 0.0) + jnp.where(place1, gate1[None, :], 0.0), axis=1
    ).reshape(expert_count, cap_pad)
    gate_hi = gate_slot.astype(BF)
    gate_lo = (gate_slot - gate_hi.astype(F32)).astype(BF)
    extra = jnp.concatenate(
        [gate_hi, gate_lo, jnp.zeros((expert_count, width - 2 * cap_pad), BF)], axis=1
    )
    buffer = dot32(placing, normed2_b).astype(BF).reshape(expert_count, cap_pad, width)
    is_extra = (jnp.arange(cap_pad) == capacity)[None, :, None]
    buffer = jnp.where(is_extra, extra[:, None, :], buffer)
    rows3 = jnp.stack(xor_all_to_all(buffer))
    info = rows3[:, capacity, :].astype(F32)
    gate_col = (info[:, :cap_pad] + info[:, cap_pad : 2 * cap_pad]).reshape(slot_total, 1)
    rows = rows3.reshape(slot_total, width)
    pre_act = dot32(rows, w_in) + b_in
    hidden, slope = gelu_both(pre_act)
    hidden_b = hidden.astype(BF)
    grad_pre = (gate_col * raw_hidden * slope).astype(BF)
    grad_part = lax.dot_general(
        grad_pre, w_in, (((1,), (1,)), ((), ())), preferred_element_type=F32
    )
    own_bias = jnp.where(tensor_id == 0, b_exp_out[0], 0.0)
    slot_grad = jnp.sum(hidden_b.astype(F32) * raw_hidden, axis=1) + jnp.sum(
        cot_rows.astype(F32) * own_bias[None, :], axis=1
    )
    slot_grad = slot_grad.reshape(expert_count, cap_pad)
    sg_hi = slot_grad.astype(BF)
    sg_lo = (slot_grad - sg_hi.astype(F32)).astype(BF)
    sg_extra = jnp.concatenate(
        [sg_hi, sg_lo, jnp.zeros((expert_count, width - 2 * cap_pad), BF)], axis=1
    )
    back = grad_part.astype(BF).reshape(expert_count, cap_pad, width)
    back = jnp.where(is_extra, sg_extra[:, None, :], back)
    grad_back3 = jnp.stack(xor_all_to_all(back))
    part_out = gate_col * (dot32(hidden_b, w_exp_out) + own_bias[None, :])
    out_back = jnp.concatenate(
        xor_all_to_all(part_out.astype(BF).reshape(expert_count, cap_pad, width))
    )
    grad_sent = (gate_col * cot_rows.astype(F32)).astype(BF)
    grad_w2 = lax.dot_general(
        hidden_b, grad_sent, (((0,), (0,)), ((), ())), preferred_element_type=F32
    ).astype(BF)
    grad_w1 = lax.dot_general(
        rows, grad_pre, (((0,), (0,)), ((), ())), preferred_element_type=F32
    ).astype(BF)
    grad_b1 = jnp.sum(grad_pre.astype(F32), axis=0)
    grad_b2 = jnp.sum(grad_sent.astype(F32), axis=0)
    w2_other = swap(grad_w2, "dp")
    w1_other = swap(grad_w1, "dp")
    biases = jnp.concatenate([grad_b1, grad_b2]).reshape(-1, 128)
    biases = (biases + swap(biases, "dp")).reshape(-1)
    grad_w_in = (grad_w1.astype(F32) + w1_other.astype(F32))[None]
    grad_w_exp_out = (grad_w2.astype(F32) + w2_other.astype(F32))[None]
    grad_b_in = biases[None, : grad_b1.shape[0]]
    grad_b_exp_out = biases[None, grad_b1.shape[0] :]
    sg_info = grad_back3[:, capacity, :].astype(F32)
    sg_col = (sg_info[:, :cap_pad] + sg_info[:, cap_pad : 2 * cap_pad]).reshape(slot_total, 1)
    gg0 = jnp.sum(jnp.where(place0, sg_col, 0.0), axis=0)
    gg1 = jnp.sum(jnp.where(place1, sg_col, 0.0), axis=0)
    gg = jnp.stack([gg0, gg1])
    gg = gg + swap(gg, "tensor")
    grad_part2 = lax.dot_general(
        placing,
        grad_back3.reshape(slot_total, width),
        (((0,), (0,)), ((), ())),
        preferred_element_type=F32,
    ).astype(BF)
    picked_sum = grad_part2.astype(F32) + swap(grad_part2, "tensor").astype(F32)
    grad_probs = (
        one_hot_f[:row_count] * gg[0][:, None] + one_hot_f[row_count:] * gg[1][:, None]
    )
    grad_logits = (
        router_probs * (grad_probs - jnp.sum(router_probs * grad_probs, axis=1, keepdims=True))
    ).astype(BF)
    grad_normed2 = picked_sum + lax.dot_general(
        grad_logits, w_router, (((1,), (1,)), ((), ())), preferred_element_type=F32
    )
    grad_router = lax.dot_general(
        normed2_b, grad_logits, (((0,), (0,)), ((), ())), preferred_element_type=F32
    )
    grad_float = cotangent.astype(F32)
    grad_ln2_scale = jnp.sum(grad_normed2 * x_hat2, axis=0)
    grad_ln2_bias = jnp.sum(grad_normed2, axis=0)
    grad_mixed = grad_float + norm_back(grad_normed2, x_hat2, inv_std2, ln2_scale)
    grad_b_out = jnp.sum(grad_mixed, axis=0)
    grad_mixed_b = grad_mixed.astype(BF)
    grad_w_out_t = lax.dot_general(
        grad_mixed_b, attended, (((0,), (0,)), ((), ())), preferred_element_type=F32
    )
    grad_w_out = reduce_dense(grad_w_out_t).T
    shard_count = 2 * group_count
    piece = width // shard_count
    small = jnp.concatenate(
        [
            grad_b_out.reshape(shard_count, piece),
            grad_ln2_scale.reshape(shard_count, piece),
            grad_ln2_bias.reshape(shard_count, piece),
            grad_router.reshape(shard_count, piece * expert_count),
        ],
        axis=1,
    )
    small = reduce_small(small)
    out_part = lax.dot_general(
        placing, out_back, (((0,), (0,)), ((), ())), preferred_element_type=F32
    ).astype(BF)
    out = (mixed + (out_part.astype(F32) + swap(out_part, "tensor").astype(F32))).astype(BF)
    grad_attended = lax.dot_general(
        grad_mixed_b, w_out, (((1,), (1,)), ((), ())), preferred_element_type=F32
    ).astype(BF)
    grad_attended = grad_attended.reshape(shape_heads)
    weights32 = jnp.exp(scores - log_sum)
    grad_values = jnp.einsum(
        "shqk,sqhe->skhe", weights32.astype(BF), grad_attended, preferred_element_type=F32
    ).astype(BF)
    grad_weights = jnp.einsum(
        "sqhe,skhe->shqk", grad_attended, value_rows, preferred_element_type=F32
    )
    delta = jnp.sum(weights32 * grad_weights, axis=-1, keepdims=True)
    grad_scores = (weights32 * (grad_weights - delta) * scaling).astype(BF)
    grad_query = jnp.einsum(
        "shqk,skhe->sqhe", grad_scores, key_rows, preferred_element_type=F32
    ).astype(BF)
    grad_keys = jnp.einsum(
        "shqk,sqhe->skhe", grad_scores, query, preferred_element_type=F32
    ).astype(BF)
    flat = (row_count, hidden_width)
    grad_qkv = jnp.concatenate(
        [grad_query.reshape(flat), grad_keys.reshape(flat), grad_values.reshape(flat)], axis=1
    )
    w_qkv_flat = w_qkv.reshape(width, 3 * hidden_width)
    grad_part1 = lax.dot_general(
        grad_qkv, w_qkv_flat, (((1,), (1,)), ((), ())), preferred_element_type=F32
    ).astype(BF)
    grad_normed1 = grad_part1.astype(F32) + swap(grad_part1, "tensor").astype(F32)
    grad_w_qkv = lax.dot_general(
        normed1_b, grad_qkv, (((0,), (0,)), ((), ())), preferred_element_type=F32
    )
    grad_w_qkv = reduce_dense(grad_w_qkv).reshape(piece, 3, hidden_width)
    grad_ln1_scale = jnp.sum(grad_normed1 * x_hat1, axis=0)
    grad_ln1_bias = jnp.sum(grad_normed1, axis=0)
    grad_tokens = (grad_mixed + norm_back(grad_normed1, x_hat1, inv_std1, ln1_scale)).astype(BF)
    small1 = reduce_small(
        jnp.concatenate(
            [
                grad_ln1_scale.reshape(shard_count, piece),
                grad_ln1_bias.reshape(shard_count, piece),
            ],
            axis=1,
        )
    )
    return (
        out,
        grad_tokens,
        small1[:piece],
        small1[piece:],
        grad_w_qkv,
        grad_w_out,
        small[:piece],
        small[piece : 2 * piece],
        small[2 * piece : 3 * piece],
        small[3 * piece :].reshape(piece, expert_count),
        grad_w_in,
        grad_b_in,
        grad_w_exp_out,
        grad_b_exp_out,
    )


def solution(mesh):
    rows = P(("dp", "expert"), None)
    shard = P(("dp", "expert"))
    placed = (
        rows,
        P(),
        P(),
        P(None, None, "tensor"),
        P("tensor", None),
        P(),
        P(),
        P(),
        P(),
        P("expert", None, "tensor"),
        P("expert", "tensor"),
        P("expert", "tensor", None),
        P("expert", None),
        rows,
        rows,
    )
    return jax.shard_map(
        per_device,
        mesh=mesh,
        in_specs=placed,
        out_specs=(
            rows,
            rows,
            shard,
            shard,
            P(("dp", "expert"), None, "tensor"),
            P("tensor", ("dp", "expert")),
            shard,
            shard,
            shard,
            rows,
            P("expert", None, "tensor"),
            P("expert", "tensor"),
            P("expert", "tensor", None),
            P("expert", None),
        ),
        check_vma=False,
    )
```

```python
import functools

import jax
import jax.numpy as jnp
from jax import lax
from jax.experimental import pallas as pl
from jax.experimental.pallas import tpu as pltpu
from jax.sharding import PartitionSpec as P

HEAD_DIM = 64
EPSILON = 1e-06
BF = jnp.bfloat16
F32 = jnp.float32
I32 = jnp.int32
LANES = 128
SCALING = HEAD_DIM ** (-0.5)

PARAMS = pltpu.CompilerParams(vmem_limit_bytes=60 * 1024 * 1024)


def round_up(value, step):
    return -(-value // step) * step


def layer_norm(values, scale, shift):
    mean_val = jnp.mean(values, axis=-1, keepdims=True)
    centred = values - mean_val
    inv_std = lax.rsqrt(jnp.mean(centred * centred, axis=-1, keepdims=True) + EPSILON)
    x_hat = centred * inv_std
    return (x_hat * scale + shift, x_hat, inv_std)


def norm_back(grad, x_hat, inv_std, scale):
    scaled = grad * scale
    return inv_std * (
        scaled
        - jnp.mean(scaled, axis=-1, keepdims=True)
        - x_hat * jnp.mean(scaled * x_hat, axis=-1, keepdims=True)
    )


def dot32(a, b):
    return jnp.dot(a, b, preferred_element_type=F32)


def dot_nt(a, b):
    return lax.dot_general(a, b, (((1,), (1,)), ((), ())), preferred_element_type=F32)


def dot_tn(a, b):
    return lax.dot_general(a, b, (((0,), (0,)), ((), ())), preferred_element_type=F32)


def iota(shape, dim):
    return lax.broadcasted_iota(I32, shape, dim)


def gelu_both(u):
    c0 = 0.7978845608028654
    square = u * u
    th = jnp.tanh(c0 * (u + 0.044715 * (square * u)))
    half = 0.5 * (1.0 + th)
    value = u * half
    slope = half + (0.5 * u) * (1.0 - th * th) * (c0 + (3.0 * 0.044715 * c0) * square)
    return value, slope


def lane_slot(cap_pad):
    lane = iota((cap_pad, LANES), 1)
    slot = iota((cap_pad, LANES), 0)
    match = (lane % cap_pad == slot) & (lane < 2 * cap_pad)
    return match, lane < cap_pad


def with_pad_row(first, column, capacity):
    cap_pad = first.shape[0]
    match, is_high = lane_slot(cap_pad)
    spread = jnp.sum(jnp.where(match, column, 0.0), axis=0, keepdims=True)
    high = spread.astype(BF).astype(F32)
    value = jnp.where(is_high, high, spread - high)
    return jnp.where(iota((cap_pad, LANES), 0) == capacity, value, first)


def from_pad_row(first, capacity):
    cap_pad = first.shape[0]
    match, _ = lane_slot(cap_pad)
    row = jnp.sum(
        jnp.where(iota((cap_pad, LANES), 0) == capacity, first, 0.0), axis=0, keepdims=True
    )
    return jnp.sum(jnp.where(match, row, 0.0), axis=1, keepdims=True)


def route_kernel(sizes, me_ref, routes_ref, cot_ref, target_ref, buffer_ref):
    rows, experts, capacity, cap_pad = sizes
    slots = experts * cap_pad
    me = me_ref[0]
    r0, r1 = routes_ref[0:1, :], routes_ref[1:2, :]
    ids = iota((experts, rows), 0)
    hot0 = jnp.where(r0 == ids, 1.0, 0.0)
    hot1 = jnp.where(r1 == ids, 1.0, 0.0)
    before = jnp.where(iota((rows, rows), 0) < iota((rows, rows), 1), 1.0, 0.0).astype(BF)
    earlier0 = dot32(hot0.astype(BF), before)
    earlier1 = dot32(hot1.astype(BF), before) + jnp.sum(hot0, axis=1, keepdims=True)
    slot0 = jnp.sum(earlier0 * hot0, axis=0, keepdims=True).astype(I32)
    slot1 = jnp.sum(earlier1 * hot1, axis=0, keepdims=True).astype(I32)
    a0 = jnp.where(slot0 < capacity, r0 * cap_pad + slot0, slots)
    a1 = jnp.where(slot1 < capacity, r1 * cap_pad + slot1, slots)
    target_ref[...] = jnp.full(target_ref.shape, slots, I32)
    target_ref[0:1, 0:rows] = a0
    target_ref[1:2, 0:rows] = a1
    target_ref[2:3, 0:rows] = jnp.where(slot0 < capacity, (r0 ^ me) * cap_pad + slot0, slots)
    target_ref[3:4, 0:rows] = jnp.where(slot1 < capacity, (r1 ^ me) * cap_pad + slot1, slots)
    ids = iota((slots, rows), 0)
    place = jnp.where((ids == a0) | (ids == a1), 1.0, 0.0).astype(BF)
    buffer_ref[...] = dot32(place, cot_ref[...]).astype(BF)


def attention_kernel(tok_ref, scale_ref, shift_ref, w_ref, att_ref, qkv_ref, lse_ref):
    normed, _, _ = layer_norm(tok_ref[...].astype(F32), scale_ref[...], shift_ref[...])
    normed = normed.astype(BF)
    rows, hidden = att_ref.shape
    for c in range(3):
        qkv_ref[c] = dot32(normed, w_ref[c]).astype(BF)
    low = iota((rows, LANES), 1) < HEAD_DIM
    for pair in range(hidden // LANES):
        cols = slice(pair * LANES, (pair + 1) * LANES)
        q, k, v = qkv_ref[0, :, cols], qkv_ref[1, :, cols], qkv_ref[2, :, cols]
        outs = []
        for part in range(2):
            mine = low if part == 0 else jnp.logical_not(low)
            scores = dot_nt(jnp.where(mine, q, jnp.zeros_like(q)), k) * SCALING
            log_sum = jnp.log(jnp.sum(jnp.exp(scores), axis=1, keepdims=True))
            weights = jnp.exp(scores - log_sum).astype(BF)
            outs.append(dot32(weights, v))
            head = 2 * pair + part
            lse_ref[:, head : head + 1] = log_sum
        att_ref[:, cols] = jnp.where(low, outs[0], outs[1]).astype(BF)


def middle_kernel(
    sizes,
    tok_ref,
    att_ref,
    att2_ref,
    w_ref,
    w2_ref,
    bias_ref,
    scale_ref,
    shift_ref,
    router_ref,
    routes_ref,
    target_ref,
    mixed_ref,
    probs_ref,
    *block_refs,
):
    rows, experts, capacity, cap_pad = sizes
    slots = experts * cap_pad
    mixed = (
        tok_ref[...].astype(F32)
        + (dot32(att_ref[...], w_ref[...]) + dot32(att2_ref[...], w2_ref[...]))
        + bias_ref[...]
    )
    mixed_ref[...] = mixed
    normed, _, _ = layer_norm(mixed, scale_ref[...], shift_ref[...])
    normed = normed.astype(BF)
    exp_logits = jnp.exp(dot_nt(router_ref[...], normed))
    probs = exp_logits / jnp.sum(exp_logits, axis=0, keepdims=True)
    probs_ref[...] = probs
    ids = iota((experts, rows), 0)
    gate0 = jnp.sum(jnp.where(routes_ref[0:1, :] == ids, probs, 0.0), axis=0, keepdims=True)
    gate1 = jnp.sum(jnp.where(routes_ref[1:2, :] == ids, probs, 0.0), axis=0, keepdims=True)
    ids = iota((slots, rows), 0)
    in0 = ids == target_ref[2:3, 0:rows]
    in1 = ids == target_ref[3:4, 0:rows]
    gates = jnp.sum(jnp.where(in0, gate0, jnp.where(in1, gate1, 0.0)), axis=1, keepdims=True)
    place = jnp.where(in0 | in1, 1.0, 0.0).astype(BF)
    for k in range(experts):
        span = slice(k * cap_pad, (k + 1) * cap_pad)
        block = dot32(place[span], normed)
        block_refs[k][:, LANES:] = block[:, LANES:].astype(BF)
        block_refs[k][:, :LANES] = with_pad_row(block[:, :LANES], gates[span], capacity).astype(BF)


def expert_kernel(
    sizes,
    me_ref,
    raw_ref,
    cot_ref,
    own_bias_ref,
    w_ref,
    b_ref,
    *refs,
):
    experts, capacity, cap_pad = sizes
    row_refs = refs[:experts]
    x_ref, gate_ref, hidden_ref, pre_ref, bsum_ref = refs[experts : experts + 5]
    back_refs = refs[experts + 5 : 2 * experts + 5]
    acc_ref, sg_ref = refs[2 * experts + 5 :]
    step, last = pl.program_id(0), pl.num_programs(0) - 1
    me = me_ref[0]

    @pl.when(step == 0)
    def _():
        acc_ref[...] = jnp.zeros_like(acc_ref)
        for k in range(experts):
            span = slice(k * cap_pad, (k + 1) * cap_pad)
            x_ref[span, :] = row_refs[k][...]
            gate = from_pad_row(row_refs[k][:, :LANES].astype(F32), capacity)
            gate_ref[span, :] = jnp.broadcast_to(gate, (cap_pad, LANES))
            cot = cot_ref[k ^ me].astype(F32)
            side = jnp.sum(cot * own_bias_ref[...], axis=1, keepdims=True)
            sg_ref[span, :] = jnp.broadcast_to(side, (cap_pad, LANES))

    w = w_ref[...]
    pre_act = dot32(x_ref[...], w) + b_ref[...]
    total = jnp.zeros(b_ref.shape, F32)
    for k in range(experts):
        span = slice(k * cap_pad, (k + 1) * cap_pad)
        value, slope = gelu_both(pre_act[span])
        raw = raw_ref[k ^ me]
        hidden_ref[span, :] = value.astype(BF)
        grad = gate_ref[span, 0:1] * raw * slope
        pre_ref[span, :] = grad.astype(BF)
        total = total + jnp.sum(grad, axis=0, keepdims=True)
        side = jnp.sum(value * raw, axis=1, keepdims=True)
        sg_ref[span, :] = sg_ref[span, :] + jnp.broadcast_to(side, (cap_pad, LANES))
    bsum_ref[...] = total
    acc_ref[...] += dot_nt(pre_ref[...], w)

    @pl.when(step == last)
    def _():
        for k in range(experts):
            span = slice(k * cap_pad, (k + 1) * cap_pad)
            back_refs[k][:, LANES:] = acc_ref[span, LANES:].astype(BF)
            first = with_pad_row(acc_ref[span, :LANES], sg_ref[span, 0:1], capacity)
            back_refs[k][:, :LANES] = first.astype(BF)


def expert_out_kernel(
    sizes, me_ref, gate_ref, cot_ref, own_bias_ref, hidden_ref, w_ref, out_ref, sent_ref, bsum_ref, acc_ref
):
    experts, capacity, cap_pad = sizes
    step, last = pl.program_id(0), pl.num_programs(0) - 1
    me = me_ref[0]

    @pl.when(step == 0)
    def _():
        acc_ref[...] = jnp.zeros_like(acc_ref)
        total = jnp.zeros(bsum_ref.shape, F32)
        for k in range(experts):
            span = slice(k * cap_pad, (k + 1) * cap_pad)
            sent = gate_ref[span, 0:1] * cot_ref[k ^ me].astype(F32)
            total = total + jnp.sum(sent, axis=0, keepdims=True)
            sent_ref[span, :] = sent.astype(BF)
        bsum_ref[...] = total

    acc_ref[...] += dot32(hidden_ref[...], w_ref[...])

    @pl.when(step == last)
    def _():
        for k in range(experts):
            span = slice(k * cap_pad, (k + 1) * cap_pad)
            value = gate_ref[span, 0:1] * (acc_ref[span, :] + own_bias_ref[...])
            out_ref[k ^ me] = value.astype(BF)


def combine_kernel(sizes, target_ref, *refs):
    rows, experts, capacity, cap_pad = sizes
    block_refs, (pack_ref, x_ref) = refs[:experts], refs[experts:]
    slots = experts * cap_pad
    lanes = target_ref.shape[1]
    body = pack_ref.shape[0] - 16
    gg0 = jnp.zeros((1, lanes), F32)
    gg1 = jnp.zeros((1, lanes), F32)
    for k in range(experts):
        span = slice(k * cap_pad, (k + 1) * cap_pad)
        x_ref[span, :] = block_refs[k][...]
        side = from_pad_row(block_refs[k][:, :LANES].astype(F32), capacity)
        ids = iota((cap_pad, lanes), 0) + k * cap_pad
        gg0 += jnp.sum(jnp.where(ids == target_ref[2:3, :], side, 0.0), axis=0, keepdims=True)
        gg1 += jnp.sum(jnp.where(ids == target_ref[3:4, :], side, 0.0), axis=0, keepdims=True)
    ids = iota((slots, lanes), 0)
    place = jnp.where(
        (ids == target_ref[2:3, :]) | (ids == target_ref[3:4, :]), 1.0, 0.0
    ).astype(BF)
    part = dot_tn(place, x_ref[...])
    pack_ref[0:body, :] = part[0:body].astype(BF)
    pack_ref[body:, :] = jnp.zeros((16, pack_ref.shape[1]), BF)
    row = iota((16, lanes), 0)
    high0, high1 = gg0.astype(BF).astype(F32), gg1.astype(BF).astype(F32)
    tail = jnp.where(
        row == 0,
        high0,
        jnp.where(row == 1, gg0 - high0, jnp.where(row == 2, high1, jnp.where(row == 3, gg1 - high1, 0.0))),
    )
    pack_ref[body:, 0:lanes] = tail.astype(BF)


def gather_out_kernel(sizes, target_ref, x_ref, out_ref):
    rows, experts, capacity, cap_pad = sizes
    ids = iota((experts * cap_pad, target_ref.shape[1]), 0)
    place = jnp.where(
        (ids == target_ref[0:1, :]) | (ids == target_ref[1:2, :]), 1.0, 0.0
    ).astype(BF)
    out_ref[...] = dot_tn(place, x_ref[...])[0 : out_ref.shape[0]].astype(BF)


def norm2_back_kernel(
    sizes,
    pack_ref,
    pack2_ref,
    mixed_ref,
    probs_ref,
    routes_ref,
    router_ref,
    cot_ref,
    scale_ref,
    shift_ref,
    att_ref,
    grad_ref,
    dense_ref,
    small_ref,
):
    rows, experts, _, _ = sizes
    hidden = att_ref.shape[1]
    body = pack_ref.shape[0] - 16
    tail = pack_ref[body:, 0:rows].astype(F32) + pack2_ref[body:, 0:rows].astype(F32)
    gg0 = tail[0:1] + tail[1:2]
    gg1 = tail[2:3] + tail[3:4]
    ids = iota((experts, rows), 0)
    grad_probs = jnp.where(routes_ref[0:1, :] == ids, gg0, 0.0) + jnp.where(
        routes_ref[1:2, :] == ids, gg1, 0.0
    )
    probs = probs_ref[...]
    grad_logits = probs * (grad_probs - jnp.sum(probs * grad_probs, axis=0, keepdims=True))
    grad_logits = grad_logits.astype(BF)
    grad_normed = (
        pack_ref[0:rows, :].astype(F32)
        + pack2_ref[0:rows, :].astype(F32)
        + dot_tn(grad_logits, router_ref[...])
    )
    normed, x_hat, inv_std = layer_norm(mixed_ref[...], scale_ref[...], shift_ref[...])
    grad_mixed = cot_ref[...].astype(F32) + norm_back(grad_normed, x_hat, inv_std, scale_ref[...])
    grad_ref[...] = grad_mixed
    dense_ref[:, 0:hidden] = dot_tn(grad_mixed.astype(BF), att_ref[...]).astype(BF)
    small_ref[...] = jnp.zeros_like(small_ref)
    small_ref[0:experts, :] = dot32(grad_logits, normed.astype(BF))
    small_ref[experts : experts + 1, :] = jnp.sum(grad_mixed, axis=0, keepdims=True)
    small_ref[experts + 1 : experts + 2, :] = jnp.sum(grad_normed * x_hat, axis=0, keepdims=True)
    small_ref[experts + 2 : experts + 3, :] = jnp.sum(grad_normed, axis=0, keepdims=True)
    dense_ref[:, hidden:] = small_ref[...].T.astype(BF)


def attention_back_kernel(
    grad_ref,
    w_out_ref,
    qkv_ref,
    lse_ref,
    tok_ref,
    scale_ref,
    shift_ref,
    w_ref,
    dense_ref,
    part_ref,
    gqkv_ref,
    small_ref,
):
    rows = tok_ref.shape[0]
    hidden = w_out_ref.shape[0]
    grad_att = dot_nt(grad_ref[...].astype(BF), w_out_ref[...]).astype(BF)
    low = iota((rows, LANES), 1) < HEAD_DIM
    for pair in range(hidden // LANES):
        cols = slice(pair * LANES, (pair + 1) * LANES)
        q, k, v = qkv_ref[0, :, cols], qkv_ref[1, :, cols], qkv_ref[2, :, cols]
        g = grad_att[:, cols]
        halves = []
        for part in range(2):
            mine = low if part == 0 else jnp.logical_not(low)
            head = 2 * pair + part
            scores = dot_nt(jnp.where(mine, q, jnp.zeros_like(q)), k) * SCALING
            weights = jnp.exp(scores - lse_ref[:, head : head + 1])
            grad_w = dot_nt(jnp.where(mine, g, jnp.zeros_like(g)), v)
            delta = jnp.sum(weights * grad_w, axis=1, keepdims=True)
            grad_s = (weights * (grad_w - delta) * SCALING).astype(BF)
            halves.append((dot32(grad_s, k), dot_tn(grad_s, q), dot_tn(weights.astype(BF), g)))
        for c in range(3):
            gqkv_ref[c, :, cols] = jnp.where(low, halves[0][c], halves[1][c]).astype(BF)
    part = dot_nt(gqkv_ref[0], w_ref[0]) + dot_nt(gqkv_ref[1], w_ref[1]) + dot_nt(gqkv_ref[2], w_ref[2])
    part_ref[...] = part.astype(BF)
    normed, x_hat, _ = layer_norm(tok_ref[...].astype(F32), scale_ref[...], shift_ref[...])
    normed = normed.astype(BF)
    for c in range(3):
        dense_ref[:, c * hidden : (c + 1) * hidden] = dot_tn(normed, gqkv_ref[c]).astype(BF)
    small_ref[...] = jnp.zeros_like(small_ref)
    small_ref[0:1, :] = jnp.sum(part * x_hat, axis=0, keepdims=True)
    small_ref[1:2, :] = jnp.sum(part, axis=0, keepdims=True)
    dense_ref[:, 3 * hidden :] = small_ref[...].T.astype(BF)


def norm1_back_kernel(part_ref, part2_ref, tok_ref, scale_ref, shift_ref, grad_ref, out_ref):
    grad = part_ref[...].astype(F32) + part2_ref[...].astype(F32)
    _, x_hat, inv_std = layer_norm(tok_ref[...].astype(F32), scale_ref[...], shift_ref[...])
    out_ref[...] = (grad_ref[...] + norm_back(grad, x_hat, inv_std, scale_ref[...])).astype(BF)


def call(kernel, outs, *args, scratch=(), scalars=0, flops=0, name=None):
    specs = [
        pl.BlockSpec(memory_space=pltpu.SMEM if i < scalars else pltpu.VMEM)
        for i in range(len(args))
    ]
    moved = sum(a.size * a.dtype.itemsize for a in args)
    return pl.pallas_call(
        kernel,
        out_shape=tuple(jax.ShapeDtypeStruct(s, d) for s, d in outs),
        in_specs=specs,
        out_specs=tuple(pl.BlockSpec(memory_space=pltpu.VMEM) for _ in outs),
        scratch_shapes=list(scratch),
        compiler_params=PARAMS,
        cost_estimate=pl.CostEstimate(flops=flops, bytes_accessed=moved, transcendentals=0),
        name=name,
    )(*args)


def swap(x, axis):
    return lax.ppermute(x, axis, [(0, 1), (1, 0)])


def xor_exchange(blocks):
    count = len(blocks)
    outs = {0: blocks[0]}
    for k in range(count - 1, 0, -1):
        outs[k] = lax.ppermute(blocks[k], "expert", [(i, i ^ k) for i in range(count)])
    return [outs[k] for k in range(count)]


def all_to_all(x):
    return lax.all_to_all(x, "expert", split_axis=0, concat_axis=0, tiled=True)


def halve(parts, axis_name, bit, index):
    size = lax.axis_size(axis_name)
    own_bit = (index // bit) % 2
    sent = lax.dynamic_index_in_dim(parts, 1 - own_bit, 0, keepdims=False)
    kept = lax.dynamic_index_in_dim(parts, own_bit, 0, keepdims=False)
    got = lax.ppermute(sent, axis_name, [(i, i ^ bit) for i in range(size)])
    return kept.astype(F32) + got.astype(F32)


def reduce_dense(part):
    count = lax.axis_size("expert")
    me = lax.axis_index("expert")
    rows = part.shape[0] // (2 * count)
    cols = part.shape[1]
    part = halve(part.reshape(2, count * rows, cols), "dp", 1, lax.axis_index("dp"))
    bit, left = 1, count
    while left > 1:
        left //= 2
        part = part.astype(BF).reshape(left, 2, rows, cols).swapaxes(0, 1)
        part = halve(part, "expert", bit, me)
        bit *= 2
    return part.reshape(rows, cols)


def per_device(
    tokens,
    ln1_scale,
    ln1_bias,
    w_qkv,
    w_out,
    b_out,
    ln2_scale,
    ln2_bias,
    w_router,
    w_in,
    b_in,
    w_exp_out,
    b_exp_out,
    routes,
    cotangent,
):
    rows, width = tokens.shape
    experts = w_router.shape[1]
    count = lax.axis_size("expert")
    me = lax.axis_index("expert").astype(I32).reshape(1)
    capacity = (5 * rows + 2 * experts - 1) // (2 * experts)
    cap_pad = round_up(capacity + 1, 16)
    slots = experts * cap_pad
    hidden = w_qkv.shape[2]
    inner = w_in.shape[2]
    lanes = round_up(rows, LANES)
    sizes = (rows, experts, capacity, cap_pad)
    esizes = (experts, capacity, cap_pad)
    w_in, w_exp_out = w_in[0], w_exp_out[0]
    w3 = w_qkv.transpose(1, 0, 2)
    router_t = w_router.T
    routes_t = routes.T
    line = lambda v: v.reshape(1, -1)
    scale1, shift1, scale2, shift2 = map(line, (ln1_scale, ln1_bias, ln2_scale, ln2_bias))

    w_out_other = swap(w_out, "tensor")
    target, cot_buffer = call(
        functools.partial(route_kernel, sizes),
        [((4, lanes), I32), ((slots, width), BF)],
        me, routes_t, cotangent,
        scalars=1, flops=2 * slots * rows * width, name="route",
    )
    cot_rows = all_to_all(cot_buffer.reshape(experts, cap_pad, width))
    attended, qkv, lse = call(
        attention_kernel,
        [((rows, hidden), BF), ((3, rows, hidden), BF), ((rows, LANES), F32)],
        tokens, scale1, shift1, w3,
        flops=6 * rows * width * hidden, name="attention",
    )
    attended_other = swap(attended, "tensor")
    mixed, probs, *blocks = call(
        functools.partial(middle_kernel, sizes),
        [((rows, width), F32), ((experts, rows), F32)] + [((cap_pad, width), BF)] * experts,
        tokens, attended, attended_other, w_out, w_out_other, line(b_out), scale2, shift2,
        router_t, routes_t, target,
        flops=4 * rows * width * hidden + 2 * slots * rows * width, name="middle",
    )
    received = xor_exchange(blocks)
    raw = dot_nt(cot_rows.reshape(slots, width), w_exp_out).reshape(experts, cap_pad, inner)
    own_bias = jnp.where(lax.axis_index("tensor") == 0, b_exp_out, 0.0)

    tile = 384
    grid = inner // tile
    whole = lambda shape: pl.BlockSpec(shape, lambda f: (0,) * len(shape))
    smem = pl.BlockSpec(memory_space=pltpu.SMEM)
    outs = pl.pallas_call(
        functools.partial(expert_kernel, esizes),
        grid=(grid,),
        out_shape=[
            jax.ShapeDtypeStruct((slots, width), BF),
            jax.ShapeDtypeStruct((slots, LANES), F32),
            jax.ShapeDtypeStruct((slots, inner), BF),
            jax.ShapeDtypeStruct((slots, inner), BF),
            jax.ShapeDtypeStruct((1, inner), F32),
        ]
        + [jax.ShapeDtypeStruct((cap_pad, width), BF)] * experts,
        in_specs=[
            smem,
            pl.BlockSpec((experts, cap_pad, tile), lambda f: (0, 0, f)),
            whole((experts, cap_pad, width)),
            whole((1, width)),
            pl.BlockSpec((width, tile), lambda f: (0, f)),
            pl.BlockSpec((1, tile), lambda f: (0, f)),
        ]
        + [whole((cap_pad, width))] * experts,
        out_specs=[
            whole((slots, width)),
            whole((slots, LANES)),
            pl.BlockSpec((slots, tile), lambda f: (0, f)),
            pl.BlockSpec((slots, tile), lambda f: (0, f)),
            pl.BlockSpec((1, tile), lambda f: (0, f)),
        ]
        + [whole((cap_pad, width))] * experts,
        scratch_shapes=[pltpu.VMEM((slots, width), F32), pltpu.VMEM((slots, LANES), F32)],
        compiler_params=PARAMS,
        cost_estimate=pl.CostEstimate(
            flops=4 * slots * width * inner, bytes_accessed=12_000_000, transcendentals=0
        ),
        name="expert",
    )(me, raw, cot_rows, own_bias, w_in, b_in, *received)
    x_rows, gate, hidden_act, grad_pre, grad_b1 = outs[:5]
    back = xor_exchange(outs[5:])
    out_rows, grad_sent, grad_b2 = pl.pallas_call(
        functools.partial(expert_out_kernel, esizes),
        grid=(grid,),
        out_shape=[
            jax.ShapeDtypeStruct((experts, cap_pad, width), BF),
            jax.ShapeDtypeStruct((slots, width), BF),
            jax.ShapeDtypeStruct((1, width), F32),
        ],
        in_specs=[
            smem,
            whole((slots, LANES)),
            whole((experts, cap_pad, width)),
            whole((1, width)),
            pl.BlockSpec((slots, tile), lambda f: (0, f)),
            pl.BlockSpec((tile, width), lambda f: (f, 0)),
        ],
        out_specs=[whole((experts, cap_pad, width)), whole((slots, width)), whole((1, width))],
        scratch_shapes=[pltpu.VMEM((slots, width), F32)],
        compiler_params=PARAMS,
        cost_estimate=pl.CostEstimate(
            flops=2 * slots * width * inner, bytes_accessed=6_000_000, transcendentals=0
        ),
        name="expert_out",
    )(me, gate, cot_rows, own_bias, hidden_act, w_exp_out)
    grad_w2 = dot_tn(hidden_act, grad_sent).astype(BF)
    grad_w1 = dot_tn(x_rows, grad_pre).astype(BF)
    w2_other = swap(grad_w2, "dp")
    w1_other = swap(grad_w1, "dp")
    biases = jnp.concatenate([grad_b1, grad_b2], axis=1)
    biases = biases + swap(biases, "dp")
    body = round_up(rows, 16)
    (pack,) = call(
        functools.partial(combine_kernel, sizes),
        [((body + 16, width), BF)],
        target, *back,
        scratch=[pltpu.VMEM((slots, width), BF)],
        flops=2 * slots * rows * width, name="combine",
    )
    pack_other = swap(pack, "tensor")
    out_rows, back0 = lax.optimization_barrier((out_rows, back[1]))
    out_back = all_to_all(out_rows)
    grad_mixed, early = call(
        functools.partial(norm2_back_kernel, sizes),
        [((rows, width), F32), ((width, hidden + LANES), BF)],
        pack, pack_other, mixed, probs, routes_t, router_t, cotangent, scale2, shift2, attended,
        scratch=[pltpu.VMEM((LANES, width), F32)],
        flops=2 * rows * width * hidden, name="norm2_back",
    )
    early = reduce_dense(early)
    late, part1 = call(
        attention_back_kernel,
        [((width, 3 * hidden + LANES), BF), ((rows, width), BF)],
        grad_mixed, w_out, qkv, lse, tokens, scale1, shift1, w3,
        scratch=[pltpu.VMEM((3, rows, hidden), BF), pltpu.VMEM((LANES, width), F32)],
        flops=14 * rows * width * hidden, name="attention_back",
    )
    part1_other = swap(part1, "tensor")
    late = reduce_dense(late)
    ln1 = late[:, 3 * hidden :]
    ln1 = ln1 + swap(ln1, "tensor")
    (grad_tokens,) = call(
        norm1_back_kernel,
        [((rows, width), BF)],
        part1, part1_other, tokens, scale1, shift1, grad_mixed,
        name="norm1_back",
    )
    (out_part,) = call(
        functools.partial(gather_out_kernel, sizes),
        [((rows, width), BF)],
        target, out_back.reshape(slots, width),
        flops=2 * slots * rows * width, name="gather_out",
    )
    out = (mixed + (out_part.astype(F32) + swap(out_part, "tensor").astype(F32))).astype(BF)
    piece = width // (2 * count)
    small = early[:, hidden:]
    return (
        out,
        grad_tokens,
        ln1[:, 0],
        ln1[:, 1],
        late[:, : 3 * hidden].reshape(piece, 3, hidden),
        early[:, :hidden].T,
        small[:, experts],
        small[:, experts + 1],
        small[:, experts + 2],
        small[:, :experts],
        (grad_w1.astype(F32) + w1_other.astype(F32))[None],
        biases[:, :inner],
        (grad_w2.astype(F32) + w2_other.astype(F32))[None],
        biases[:, inner:],
    )


def solution(mesh):
    rows = P(("dp", "expert"), None)
    shard = P(("dp", "expert"))
    placed = (
        rows,
        P(),
        P(),
        P(None, None, "tensor"),
        P("tensor", None),
        P(),
        P(),
        P(),
        P(),
        P("expert", None, "tensor"),
        P("expert", "tensor"),
        P("expert", "tensor", None),
        P("expert", None),
        rows,
        rows,
    )
    return jax.shard_map(
        per_device,
        mesh=mesh,
        in_specs=placed,
        out_specs=(
            rows,
            rows,
            shard,
            shard,
            P(("dp", "expert"), None, "tensor"),
            P("tensor", ("dp", "expert")),
            shard,
            shard,
            shard,
            rows,
            P("expert", None, "tensor"),
            P("expert", "tensor"),
            P("expert", "tensor", None),
            P("expert", None),
        ),
        check_vma=False,
    )
```

```python
import functools

import jax
import jax.numpy as jnp
from jax import lax
from jax.experimental import pallas as pl
from jax.experimental.pallas import tpu as pltpu
from jax.sharding import PartitionSpec as P


HEAD_DIM = 64
EPSILON = 1e-06
BF = jnp.bfloat16
F32 = jnp.float32
I32 = jnp.int32
LANES = 128
SCALING = HEAD_DIM ** (-0.5)

PARAMS = pltpu.CompilerParams(vmem_limit_bytes=60 * 1024 * 1024)


def round_up(value, step):
    return -(-value // step) * step


def layer_norm(values, scale, shift):
    mean_val = jnp.mean(values, axis=-1, keepdims=True)
    centred = values - mean_val
    inv_std = lax.rsqrt(jnp.mean(centred * centred, axis=-1, keepdims=True) + EPSILON)
    x_hat = centred * inv_std
    return (x_hat * scale + shift, x_hat, inv_std)


def norm_back(grad, x_hat, inv_std, scale):
    scaled = grad * scale
    return inv_std * (
        scaled
        - jnp.mean(scaled, axis=-1, keepdims=True)
        - x_hat * jnp.mean(scaled * x_hat, axis=-1, keepdims=True)
    )


def dot32(a, b):
    return jnp.dot(a, b, preferred_element_type=F32)


def dot_nt(a, b):
    return lax.dot_general(a, b, (((1,), (1,)), ((), ())), preferred_element_type=F32)


def dot_tn(a, b):
    return lax.dot_general(a, b, (((0,), (0,)), ((), ())), preferred_element_type=F32)


def iota(shape, dim):
    return lax.broadcasted_iota(I32, shape, dim)


def gelu_both(u):
    c0 = 0.7978845608028654
    square = u * u
    th = jnp.tanh(u * (c0 + (0.044715 * c0) * square))
    half = 0.5 + 0.5 * th
    value = u * half
    slope = half + value * (1.0 - th) * (c0 + (3.0 * 0.044715 * c0) * square)
    return value, slope


def lane_slot(cap_pad):
    lane = iota((cap_pad, LANES), 1)
    slot = iota((cap_pad, LANES), 0)
    match = (lane % cap_pad == slot) & (lane < 2 * cap_pad)
    return match, lane < cap_pad


def with_pad_row(first, column, capacity):
    cap_pad = first.shape[0]
    match, is_high = lane_slot(cap_pad)
    spread = jnp.sum(jnp.where(match, column, 0.0), axis=0, keepdims=True)
    high = spread.astype(BF).astype(F32)
    value = jnp.where(is_high, high, spread - high)
    return jnp.where(iota((cap_pad, LANES), 0) == capacity, value, first)


def from_pad_row(first, capacity):
    cap_pad = first.shape[0]
    match, _ = lane_slot(cap_pad)
    row = jnp.sum(
        jnp.where(iota((cap_pad, LANES), 0) == capacity, first, 0.0), axis=0, keepdims=True
    )
    return jnp.sum(jnp.where(match, row, 0.0), axis=1, keepdims=True)


def row(ref):
    return ref[...].reshape(1, -1)


def route_kernel(sizes, ids_ref, routes_ref, cot_ref, target_ref, buffer_ref):
    rows, experts, capacity, cap_pad = sizes
    slots = experts * cap_pad
    me = ids_ref[0]
    r0, r1 = routes_ref[0:1, :], routes_ref[1:2, :]
    ids = iota((experts, rows), 0)
    hot0 = jnp.where(r0 == ids, 1.0, 0.0)
    hot1 = jnp.where(r1 == ids, 1.0, 0.0)
    before = jnp.where(iota((rows, rows), 0) < iota((rows, rows), 1), 1.0, 0.0).astype(BF)
    earlier0 = dot32(hot0.astype(BF), before)
    earlier1 = dot32(hot1.astype(BF), before) + jnp.sum(hot0, axis=1, keepdims=True)
    slot0 = jnp.sum(earlier0 * hot0, axis=0, keepdims=True).astype(I32)
    slot1 = jnp.sum(earlier1 * hot1, axis=0, keepdims=True).astype(I32)
    a0 = jnp.where(slot0 < capacity, r0 * cap_pad + slot0, slots)
    a1 = jnp.where(slot1 < capacity, r1 * cap_pad + slot1, slots)
    target_ref[...] = jnp.full(target_ref.shape, slots, I32)
    target_ref[0:1, 0:rows] = a0
    target_ref[1:2, 0:rows] = a1
    target_ref[2:3, 0:rows] = jnp.where(slot0 < capacity, (r0 ^ me) * cap_pad + slot0, slots)
    target_ref[3:4, 0:rows] = jnp.where(slot1 < capacity, (r1 ^ me) * cap_pad + slot1, slots)
    ids = iota((slots, rows), 0)
    place = jnp.where((ids == a0) | (ids == a1), 1.0, 0.0).astype(BF)
    buffer_ref[...] = dot32(place, cot_ref[...]).astype(BF)


def attention_kernel(
    tok_ref, scale_ref, shift_ref, w_ref, w_out_ref, part_ref, att_ref, qkv_ref, lse_ref
):
    normed, _, _ = layer_norm(tok_ref[...].astype(F32), row(scale_ref), row(shift_ref))
    normed = normed.astype(BF)
    rows, hidden = att_ref.shape
    for c in range(3):
        qkv_ref[c] = dot32(normed, w_ref[c]).astype(BF)
    low = iota((rows, LANES), 1) < HEAD_DIM
    for pair in range(hidden // LANES):
        cols = slice(pair * LANES, (pair + 1) * LANES)
        q, k, v = qkv_ref[0, :, cols], qkv_ref[1, :, cols], qkv_ref[2, :, cols]
        outs = []
        for part in range(2):
            mine = low if part == 0 else jnp.logical_not(low)
            scores = dot_nt(jnp.where(mine, q, jnp.zeros_like(q)), k) * SCALING
            log_sum = jnp.log(jnp.sum(jnp.exp(scores), axis=1, keepdims=True))
            weights = jnp.exp(scores - log_sum).astype(BF)
            outs.append(dot32(weights, v))
            head = 2 * pair + part
            lse_ref[:, head : head + 1] = log_sum
        att_ref[:, cols] = jnp.where(low, outs[0], outs[1]).astype(BF)
    part_ref[...] = dot32(att_ref[...], w_out_ref[...]).astype(BF)


def middle_kernel(
    sizes,
    tok_ref,
    part_ref,
    part2_ref,
    bias_ref,
    scale_ref,
    shift_ref,
    router_ref,
    routes_ref,
    target_ref,
    mixed_ref,
    probs_ref,
    *block_refs,
):
    rows, experts, capacity, cap_pad = sizes
    slots = experts * cap_pad
    mixed = (
        tok_ref[...].astype(F32)
        + (part_ref[...].astype(F32) + part2_ref[...].astype(F32))
        + row(bias_ref)
    )
    mixed_ref[...] = mixed
    normed, _, _ = layer_norm(mixed, row(scale_ref), row(shift_ref))
    normed = normed.astype(BF)
    exp_logits = jnp.exp(dot_nt(router_ref[...], normed))
    probs = exp_logits / jnp.sum(exp_logits, axis=0, keepdims=True)
    probs_ref[...] = probs
    ids = iota((experts, rows), 0)
    gate0 = jnp.sum(jnp.where(routes_ref[0:1, :] == ids, probs, 0.0), axis=0, keepdims=True)
    gate1 = jnp.sum(jnp.where(routes_ref[1:2, :] == ids, probs, 0.0), axis=0, keepdims=True)
    ids = iota((slots, rows), 0)
    in0 = ids == target_ref[2:3, 0:rows]
    in1 = ids == target_ref[3:4, 0:rows]
    gates = jnp.sum(jnp.where(in0, gate0, jnp.where(in1, gate1, 0.0)), axis=1, keepdims=True)
    place = jnp.where(in0 | in1, 1.0, 0.0).astype(BF)
    for k in range(experts):
        span = slice(k * cap_pad, (k + 1) * cap_pad)
        block = dot32(place[span], normed)
        block_refs[k][:, LANES:] = block[:, LANES:].astype(BF)
        block_refs[k][:, :LANES] = with_pad_row(block[:, :LANES], gates[span], capacity).astype(BF)


def expert_kernel(sizes, ids_ref, raw_ref, cot_ref, bias2_ref, w_ref, b_ref, *refs):
    blocks, capacity, cap_pad, held, base = sizes
    row_refs = refs[:blocks]
    x_ref, gate_ref, hidden_ref, pre_ref, bsum_ref = refs[blocks + held : blocks + held + 5]
    back_refs = refs[blocks + held + 5 : 2 * blocks + held + 5]
    acc_ref, sg_ref = refs[2 * blocks + held + 5 :]
    step, last = pl.program_id(0), pl.num_programs(0) - 1

    @pl.when(step == 0)
    def _():
        acc_ref[...] = jnp.zeros_like(acc_ref)
        first = jnp.where(ids_ref[1] == 0, 1.0, 0.0)
        for k in range(blocks):
            span = slice(k * cap_pad, (k + 1) * cap_pad)
            x_ref[span, :] = row_refs[k][...]
            gate = from_pad_row(row_refs[k][:, :LANES].astype(F32), capacity)
            gate_ref[span, :] = jnp.broadcast_to(gate, (cap_pad, LANES))
            cot = cot_ref[(base + k) ^ ids_ref[0]].astype(F32)
            side = jnp.sum(cot * bias2_ref[...], axis=1, keepdims=True)
            sg_ref[span, :] = jnp.broadcast_to(first * side, (cap_pad, LANES))

    w = w_ref[...]
    pre_act = dot32(x_ref[...], w) + b_ref[...]
    total = jnp.zeros(b_ref.shape, F32)
    for k in range(blocks):
        span = slice(k * cap_pad, (k + 1) * cap_pad)
        value, slope = gelu_both(pre_act[span])
        raw = raw_ref[(base + k) ^ ids_ref[0]]
        hidden_ref[span, :] = value.astype(BF)
        grad = gate_ref[span, 0:1] * raw * slope
        pre_ref[span, :] = grad.astype(BF)
        total = total + jnp.sum(grad, axis=0, keepdims=True)
        side = jnp.sum(value * raw, axis=1, keepdims=True)
        sg_ref[span, :] = sg_ref[span, :] + jnp.broadcast_to(side, (cap_pad, LANES))
    bsum_ref[...] = total
    acc_ref[...] += dot_nt(pre_ref[...], w)

    @pl.when(step == last)
    def _():
        for k in range(blocks):
            span = slice(k * cap_pad, (k + 1) * cap_pad)
            back_refs[k][:, LANES:] = acc_ref[span, LANES:].astype(BF)
            first = with_pad_row(acc_ref[span, :LANES], sg_ref[span, 0:1], capacity)
            back_refs[k][:, :LANES] = first.astype(BF)


def expert_out_kernel(
    sizes, ids_ref, gate_ref, cot_ref, bias2_ref, hidden_ref, w_ref, out_ref, sent_ref, bsum_ref, acc_ref
):
    experts, _, cap_pad = sizes
    step, last = pl.program_id(0), pl.num_programs(0) - 1

    @pl.when(step == 0)
    def _():
        acc_ref[...] = jnp.zeros_like(acc_ref)
        total = jnp.zeros(bsum_ref.shape, F32)
        for k in range(experts):
            span = slice(k * cap_pad, (k + 1) * cap_pad)
            sent = gate_ref[span, 0:1] * cot_ref[k ^ ids_ref[0]].astype(F32)
            total = total + jnp.sum(sent, axis=0, keepdims=True)
            sent_ref[span, :] = sent.astype(BF)
        bsum_ref[...] = total

    acc_ref[...] += dot32(hidden_ref[...], w_ref[...])

    @pl.when(step == last)
    def _():
        bias = jnp.where(ids_ref[1] == 0, 1.0, 0.0) * bias2_ref[...]
        for k in range(experts):
            span = slice(k * cap_pad, (k + 1) * cap_pad)
            value = gate_ref[span, 0:1] * (acc_ref[span, :] + bias)
            out_ref[k ^ ids_ref[0]] = value.astype(BF)


def combine_kernel(sizes, target_ref, *refs):
    _, experts, capacity, cap_pad = sizes
    block_refs, (pack_ref, x_ref) = refs[:experts], refs[experts:]
    slots = experts * cap_pad
    lanes = target_ref.shape[1]
    body = pack_ref.shape[0] - 16
    gg0 = jnp.zeros((1, lanes), F32)
    gg1 = jnp.zeros((1, lanes), F32)
    for k in range(experts):
        span = slice(k * cap_pad, (k + 1) * cap_pad)
        x_ref[span, :] = block_refs[k][...]
        side = from_pad_row(block_refs[k][:, :LANES].astype(F32), capacity)
        ids = iota((cap_pad, lanes), 0) + k * cap_pad
        gg0 += jnp.sum(jnp.where(ids == target_ref[2:3, :], side, 0.0), axis=0, keepdims=True)
        gg1 += jnp.sum(jnp.where(ids == target_ref[3:4, :], side, 0.0), axis=0, keepdims=True)
    ids = iota((slots, lanes), 0)
    place = jnp.where(
        (ids == target_ref[2:3, :]) | (ids == target_ref[3:4, :]), 1.0, 0.0
    ).astype(BF)
    part = dot_tn(place, x_ref[...])
    pack_ref[0:body, :] = part[0:body].astype(BF)
    pack_ref[body:, :] = jnp.zeros((16, pack_ref.shape[1]), BF)
    line = iota((16, lanes), 0)
    high0, high1 = gg0.astype(BF).astype(F32), gg1.astype(BF).astype(F32)
    tail = jnp.where(line == 0, high0, jnp.where(line == 1, gg0 - high0, 0.0))
    tail = jnp.where(line == 2, high1, jnp.where(line == 3, gg1 - high1, tail))
    pack_ref[body:, 0:lanes] = tail.astype(BF)


def gather_out_kernel(sizes, target_ref, x_ref, out_ref):
    _, experts, _, cap_pad = sizes
    ids = iota((experts * cap_pad, target_ref.shape[1]), 0)
    place = jnp.where(
        (ids == target_ref[0:1, :]) | (ids == target_ref[1:2, :]), 1.0, 0.0
    ).astype(BF)
    out_ref[...] = dot_tn(place, x_ref[...])[0 : out_ref.shape[0]].astype(BF)


def halves(ids_ref, width):
    half = width // 2
    return (
        pl.ds(pl.multiple_of(ids_ref[2] * half, LANES), half),
        pl.ds(pl.multiple_of((1 - ids_ref[2]) * half, LANES), half),
    )


def norm2_back_kernel(
    sizes,
    ids_ref,
    pack_ref,
    pack2_ref,
    mixed_ref,
    probs_ref,
    routes_ref,
    router_ref,
    cot_ref,
    scale_ref,
    shift_ref,
    att_ref,
    w_out_ref,
    qkv_ref,
    lse_ref,
    tok_ref,
    scale1_ref,
    shift1_ref,
    grad_ref,
    grad_att_ref,
    grad_v_ref,
    keep_ref,
    send_ref,
    small_ref,
    left_ref,
):
    rows, experts, _, _ = sizes
    width = tok_ref.shape[1]
    hidden = att_ref.shape[1]
    body = pack_ref.shape[0] - 16
    tail = pack_ref[body:, 0:rows].astype(F32) + pack2_ref[body:, 0:rows].astype(F32)
    gg0 = tail[0:1] + tail[1:2]
    gg1 = tail[2:3] + tail[3:4]
    ids = iota((experts, rows), 0)
    grad_probs = jnp.where(routes_ref[0:1, :] == ids, gg0, 0.0) + jnp.where(
        routes_ref[1:2, :] == ids, gg1, 0.0
    )
    probs = probs_ref[...]
    grad_logits = probs * (grad_probs - jnp.sum(probs * grad_probs, axis=0, keepdims=True))
    grad_logits = grad_logits.astype(BF)
    grad_normed = (
        pack_ref[0:rows, :].astype(F32)
        + pack2_ref[0:rows, :].astype(F32)
        + dot_tn(grad_logits, router_ref[...])
    )
    normed, x_hat, inv_std = layer_norm(mixed_ref[...], row(scale_ref), row(shift_ref))
    grad_mixed = cot_ref[...].astype(F32) + norm_back(grad_normed, x_hat, inv_std, row(scale_ref))
    grad_ref[...] = grad_mixed
    left_ref[...] = grad_mixed.astype(BF)
    sides = tuple(zip((keep_ref, send_ref), halves(ids_ref, width)))
    for ref, cols in sides:
        ref[:, 0:hidden] = dot_tn(left_ref[:, cols], att_ref[...]).astype(BF)
    small_ref[...] = jnp.zeros_like(small_ref)
    small_ref[0:experts, :] = dot32(grad_logits, normed.astype(BF))
    small_ref[experts : experts + 1, :] = jnp.sum(grad_mixed, axis=0, keepdims=True)
    small_ref[experts + 1 : experts + 2, :] = jnp.sum(grad_normed * x_hat, axis=0, keepdims=True)
    small_ref[experts + 2 : experts + 3, :] = jnp.sum(grad_normed, axis=0, keepdims=True)
    for ref, cols in sides:
        ref[:, 2 * hidden :] = small_ref[:, cols].T.astype(BF)
    grad_att_ref[...] = dot_nt(left_ref[...], w_out_ref[...]).astype(BF)
    low = iota((rows, LANES), 1) < HEAD_DIM
    for pair in range(hidden // LANES):
        cols = slice(pair * LANES, (pair + 1) * LANES)
        q, k = qkv_ref[0, :, cols], qkv_ref[1, :, cols]
        g = grad_att_ref[:, cols]
        outs = []
        for part in range(2):
            mine = low if part == 0 else jnp.logical_not(low)
            head = 2 * pair + part
            scores = dot_nt(jnp.where(mine, q, jnp.zeros_like(q)), k) * SCALING
            weights = jnp.exp(scores - lse_ref[:, head : head + 1])
            outs.append(dot_tn(weights.astype(BF), g))
        grad_v_ref[:, cols] = jnp.where(low, outs[0], outs[1]).astype(BF)
    normed1, _, _ = layer_norm(tok_ref[...].astype(F32), row(scale1_ref), row(shift1_ref))
    left_ref[...] = normed1.astype(BF)
    for ref, cols in sides:
        ref[:, hidden : 2 * hidden] = dot_tn(left_ref[:, cols], grad_v_ref[...]).astype(BF)


def attention_back_kernel(
    ids_ref,
    grad_att_ref,
    grad_v_ref,
    qkv_ref,
    lse_ref,
    tok_ref,
    scale_ref,
    shift_ref,
    w_ref,
    part_ref,
    keep_ref,
    send_ref,
    gqk_ref,
    small_ref,
    left_ref,
):
    rows, width = tok_ref.shape
    hidden = grad_att_ref.shape[1]
    low = iota((rows, LANES), 1) < HEAD_DIM
    for pair in range(hidden // LANES):
        cols = slice(pair * LANES, (pair + 1) * LANES)
        q, k, v = qkv_ref[0, :, cols], qkv_ref[1, :, cols], qkv_ref[2, :, cols]
        g = grad_att_ref[:, cols]
        outs = []
        for part in range(2):
            mine = low if part == 0 else jnp.logical_not(low)
            head = 2 * pair + part
            scores = dot_nt(jnp.where(mine, q, jnp.zeros_like(q)), k) * SCALING
            weights = jnp.exp(scores - lse_ref[:, head : head + 1])
            grad_w = dot_nt(jnp.where(mine, g, jnp.zeros_like(g)), v)
            delta = jnp.sum(weights * grad_w, axis=1, keepdims=True)
            grad_s = (weights * (grad_w - delta) * SCALING).astype(BF)
            outs.append((dot32(grad_s, k), dot_tn(grad_s, q)))
        for c in range(2):
            gqk_ref[c, :, cols] = jnp.where(low, outs[0][c], outs[1][c]).astype(BF)
    part = dot_nt(gqk_ref[0], w_ref[0]) + dot_nt(gqk_ref[1], w_ref[1]) + dot_nt(grad_v_ref[...], w_ref[2])
    part_ref[...] = part.astype(BF)
    normed, x_hat, _ = layer_norm(tok_ref[...].astype(F32), row(scale_ref), row(shift_ref))
    left_ref[...] = normed.astype(BF)
    small_ref[...] = jnp.zeros_like(small_ref)
    small_ref[0:1, :] = jnp.sum(part * x_hat, axis=0, keepdims=True)
    small_ref[1:2, :] = jnp.sum(part, axis=0, keepdims=True)
    for ref, cols in zip((keep_ref, send_ref), halves(ids_ref, width)):
        for c in range(2):
            ref[:, c * hidden : (c + 1) * hidden] = dot_tn(left_ref[:, cols], gqk_ref[c]).astype(BF)
        ref[:, 2 * hidden :] = small_ref[:, cols].T.astype(BF)


def norm1_back_kernel(part_ref, part2_ref, tok_ref, scale_ref, shift_ref, grad_ref, out_ref):
    grad = part_ref[...].astype(F32) + part2_ref[...].astype(F32)
    _, x_hat, inv_std = layer_norm(tok_ref[...].astype(F32), row(scale_ref), row(shift_ref))
    out_ref[...] = (grad_ref[...] + norm_back(grad, x_hat, inv_std, row(scale_ref))).astype(BF)


def hop_kernel(bit, ids_ref, kept_ref, got_ref, keep_ref, send_ref):
    mine = (ids_ref[0] >> bit) & 1
    for j in range(keep_ref.shape[0]):
        a, b = 2 * j + mine, 2 * j + 1 - mine
        keep_ref[j] = (kept_ref[a].astype(F32) + got_ref[a].astype(F32)).astype(BF)
        send_ref[j] = (kept_ref[b].astype(F32) + got_ref[b].astype(F32)).astype(BF)


def early_end_kernel(part_ref, w_out_ref, v_ref, small_ref):
    hidden = v_ref.shape[1]
    total = part_ref[0].astype(F32)
    for k in range(1, part_ref.shape[0]):
        total = total + part_ref[k].astype(F32)
    w_out_ref[...] = total[:, :hidden]
    v_ref[...] = total[:, hidden : 2 * hidden]
    small_ref[...] = total[:, 2 * hidden :]


def late_end_kernel(kept_ref, got_ref, v_ref, qkv_ref, ln1_ref):
    hidden = v_ref.shape[1]
    total = kept_ref[0].astype(F32) + got_ref[0].astype(F32)
    qkv_ref[0] = total[:, :hidden]
    qkv_ref[1] = total[:, hidden : 2 * hidden]
    qkv_ref[2] = v_ref[...]
    ln1_ref[...] = total[:, 2 * hidden :]


def weight_grad_kernel(ids_ref, a_ref, a2_ref, b_ref, b2_ref, out_ref):
    @pl.when(ids_ref[2] == 0)
    def _():
        out_ref[...] = dot_tn(a_ref[...], b_ref[...]) + dot_tn(a2_ref[...], b2_ref[...])

    @pl.when(ids_ref[2] == 1)
    def _():
        out_ref[...] = dot_tn(a2_ref[...], b2_ref[...]) + dot_tn(a_ref[...], b_ref[...])


def weight_grad(ids, a, a2, b, b2):
    slots, rows = a.shape
    cols = b.shape[1]
    tile = 512 if rows % 512 == 0 and rows > cols else 256
    left = pl.BlockSpec((slots, tile), lambda i: (0, i))
    right = pl.BlockSpec((slots, cols), lambda i: (0, 0))
    return pl.pallas_call(
        weight_grad_kernel,
        grid=(rows // tile,),
        out_shape=jax.ShapeDtypeStruct((rows, cols), F32),
        in_specs=[pl.BlockSpec(memory_space=pltpu.SMEM), left, left, right, right],
        out_specs=pl.BlockSpec((tile, cols), lambda i: (i, 0)),
        compiler_params=PARAMS,
        cost_estimate=pl.CostEstimate(
            flops=4 * slots * rows * cols, bytes_accessed=9_000_000, transcendentals=0
        ),
    )(ids, a, a2, b, b2)


def call(kernel, outs, *args, scratch=(), scalars=0, flops=0):
    specs = [
        pl.BlockSpec(memory_space=pltpu.SMEM if i < scalars else pltpu.VMEM)
        for i in range(len(args))
    ]
    moved = sum(a.size * a.dtype.itemsize for a in args)
    return pl.pallas_call(
        kernel,
        out_shape=tuple(jax.ShapeDtypeStruct(s, d) for s, d in outs),
        in_specs=specs,
        out_specs=tuple(pl.BlockSpec(memory_space=pltpu.VMEM) for _ in outs),
        scratch_shapes=list(scratch),
        compiler_params=PARAMS,
        cost_estimate=pl.CostEstimate(flops=flops, bytes_accessed=moved, transcendentals=0),
    )(*args)


def swap(x, axis):
    return lax.ppermute(x, axis, [(0, 1), (1, 0)])


def xor_exchange(blocks, count, order):
    outs = {}
    for k in order:
        outs[k] = lax.ppermute(blocks[k], "expert", [(i, i ^ k) for i in range(count)])
    return outs


def all_to_all(x):
    return lax.all_to_all(x, "expert", split_axis=0, concat_axis=0, tiled=True)


def reduce_dense(ids, keep, send):
    count = lax.axis_size("expert")
    piece = keep.shape[0] // count
    cols = keep.shape[1]
    got = swap(send, "dp").reshape(count, piece, cols)
    keep = keep.reshape(count, piece, cols)
    bit, left = 0, count
    while left > 1:
        left //= 2
        keep, send = call(
            functools.partial(hop_kernel, bit),
            [((left, piece, cols), BF), ((left, piece, cols), BF)],
            ids, keep, got,
            scalars=1,
        )
        got = lax.ppermute(send, "expert", [(i, i ^ (1 << bit)) for i in range(count)])
        bit += 1
    return keep, got


def per_device(
    tokens,
    ln1_scale,
    ln1_bias,
    w_qkv,
    w_out,
    b_out,
    ln2_scale,
    ln2_bias,
    w_router,
    w_in,
    b_in,
    w_exp_out,
    b_exp_out,
    routes,
    cotangent,
):
    rows, width = tokens.shape
    experts = w_router.shape[1]
    count = lax.axis_size("expert")
    ids = jnp.stack(
        [lax.axis_index("expert"), lax.axis_index("tensor"), lax.axis_index("dp")]
    ).astype(I32)
    capacity = (5 * rows + 2 * experts - 1) // (2 * experts)
    cap_pad = round_up(capacity + 1, 16)
    slots = experts * cap_pad
    hidden = w_qkv.shape[2]
    inner = w_in.shape[2]
    lanes = round_up(rows, LANES)
    half = width // 2
    sizes = (rows, experts, capacity, cap_pad)
    w_in, w_exp_out = w_in[0], w_exp_out[0]
    w3 = w_qkv.transpose(1, 0, 2)
    router_t = w_router.T
    routes_t = routes.T

    target, cot_buffer = call(
        functools.partial(route_kernel, sizes),
        [((4, lanes), I32), ((slots, width), BF)],
        ids, routes_t, cotangent,
        scalars=1, flops=2 * slots * rows * width,
    )
    cot_rows = all_to_all(cot_buffer.reshape(experts, cap_pad, width))
    part, attended, qkv, lse = call(
        attention_kernel,
        [((rows, width), BF), ((rows, hidden), BF), ((3, rows, hidden), BF), ((rows, LANES), F32)],
        tokens, ln1_scale, ln1_bias, w3, w_out,
        flops=8 * rows * width * hidden,
    )
    part_other = swap(part, "tensor")
    mixed, probs, *blocks = call(
        functools.partial(middle_kernel, sizes),
        [((rows, width), F32), ((experts, rows), F32)] + [((cap_pad, width), BF)] * experts,
        tokens, part, part_other, b_out, ln2_scale, ln2_bias, router_t, routes_t, target,
        flops=2 * slots * rows * width,
    )
    near = experts
    order = tuple(range(experts - 1, 0, -1))
    received = xor_exchange(blocks, count, order)
    received[0] = blocks[0]

    tile = 384
    grid = inner // tile
    whole = lambda shape: pl.BlockSpec(shape, lambda f: (0,) * len(shape))
    smem = pl.BlockSpec(memory_space=pltpu.SMEM)
    anywhere = pl.BlockSpec(memory_space=pl.ANY)
    raw = dot_nt(cot_rows.reshape(slots, width), w_exp_out).reshape(experts, cap_pad, inner)

    def expert(which, held):
        span = near * cap_pad
        at = lambda f: (which, f)
        fixed = lambda f: (which, 0)
        shapes = [
            jax.ShapeDtypeStruct((slots, width), BF),
            jax.ShapeDtypeStruct((slots, LANES), F32),
            jax.ShapeDtypeStruct((slots, inner), BF),
            jax.ShapeDtypeStruct((slots, inner), BF),
        ]
        return pl.pallas_call(
            functools.partial(expert_kernel, (near, capacity, cap_pad, len(held), which * near)),
            grid=(grid,),
            out_shape=shapes
            + [jax.ShapeDtypeStruct((1, inner), F32)]
            + [jax.ShapeDtypeStruct((cap_pad, width), BF)] * near,
            in_specs=[
                smem,
                pl.BlockSpec((experts, cap_pad, tile), lambda f: (0, 0, f)),
                whole((experts, cap_pad, width)),
                whole((1, width)),
                pl.BlockSpec((width, tile), lambda f: (0, f)),
                pl.BlockSpec((1, tile), lambda f: (0, f)),
            ]
            + [whole((cap_pad, width))] * near
            + [anywhere] * len(held),
            out_specs=[
                pl.BlockSpec((span, width), fixed),
                pl.BlockSpec((span, LANES), fixed),
                pl.BlockSpec((span, tile), at),
                pl.BlockSpec((span, tile), at),
                pl.BlockSpec((1, tile), lambda f: (0, f)),
            ]
            + [whole((cap_pad, width))] * near,
            input_output_aliases={6 + near + i: i for i in range(len(held))},
            scratch_shapes=[pltpu.VMEM((span, width), F32), pltpu.VMEM((span, LANES), F32)],
            compiler_params=PARAMS,
            cost_estimate=pl.CostEstimate(
                flops=2 * slots * width * inner, bytes_accessed=6_000_000, transcendentals=0
            ),
        )(
            ids, raw, cot_rows, b_exp_out, w_in, b_in,
            *[received[which * near + i] for i in range(near)],
            *held,
        )

    outs = expert(0, ())
    x_rows, gate, hidden_act, grad_pre, grad_b1 = outs[:5]
    back = xor_exchange(outs[5:], count, order)
    back[0] = outs[5]
    out_rows, grad_sent, grad_b2 = pl.pallas_call(
        functools.partial(expert_out_kernel, (experts, capacity, cap_pad)),
        grid=(grid,),
        out_shape=[
            jax.ShapeDtypeStruct((experts, cap_pad, width), BF),
            jax.ShapeDtypeStruct((slots, width), BF),
            jax.ShapeDtypeStruct((1, width), F32),
        ],
        in_specs=[
            smem,
            whole((slots, LANES)),
            whole((experts, cap_pad, width)),
            whole((1, width)),
            pl.BlockSpec((slots, tile), lambda f: (0, f)),
            pl.BlockSpec((tile, width), lambda f: (f, 0)),
        ],
        out_specs=[whole((experts, cap_pad, width)), whole((slots, width)), whole((1, width))],
        scratch_shapes=[pltpu.VMEM((slots, width), F32)],
        compiler_params=PARAMS,
        cost_estimate=pl.CostEstimate(
            flops=2 * slots * width * inner, bytes_accessed=6_000_000, transcendentals=0
        ),
        name="expert_out",
    )(ids, gate, cot_rows, b_exp_out, hidden_act, w_exp_out)
    x_other = swap(x_rows, "dp")
    pre_other = swap(grad_pre, "dp")
    hidden_other = swap(hidden_act, "dp")
    sent_other = swap(grad_sent, "dp")
    grad_w_in = weight_grad(ids, x_rows, x_other, grad_pre, pre_other)
    grad_w_exp_out = weight_grad(ids, hidden_act, hidden_other, grad_sent, sent_other)
    biases = jnp.concatenate([grad_b1, grad_b2], axis=1)
    biases = biases + swap(biases, "dp")
    body = round_up(rows, 16)
    target, out_rows = lax.optimization_barrier((target, out_rows))
    (pack,) = call(
        functools.partial(combine_kernel, sizes),
        [((body + 16, width), BF)],
        target, *[back[k] for k in range(experts)],
        scratch=[pltpu.VMEM((slots, width), BF)],
        flops=2 * slots * rows * width,
    )
    pack_other = swap(pack, "tensor")
    out_rows, pack = lax.optimization_barrier((out_rows, pack))
    out_back = all_to_all(out_rows)
    grad_mixed, grad_att, grad_v, keep, send = call(
        functools.partial(norm2_back_kernel, sizes),
        [
            ((rows, width), F32),
            ((rows, hidden), BF),
            ((rows, hidden), BF),
            ((half, 2 * hidden + LANES), BF),
            ((half, 2 * hidden + LANES), BF),
        ],
        ids, pack, pack_other, mixed, probs, routes_t, router_t, cotangent, ln2_scale,
        ln2_bias, attended, w_out, qkv, lse, tokens, ln1_scale, ln1_bias,
        scratch=[pltpu.VMEM((LANES, width), F32), pltpu.VMEM((rows, width), BF)],
        scalars=1, flops=8 * rows * width * hidden,
    )
    piece = half // count
    got = swap(send, "dp")
    early = (keep.astype(F32) + got.astype(F32)).astype(BF)
    early = all_to_all(early.reshape(count, piece, -1))
    part1, keep, send = call(
        attention_back_kernel,
        [((rows, width), BF), ((half, 2 * hidden + LANES), BF), ((half, 2 * hidden + LANES), BF)],
        ids, grad_att, grad_v, qkv, lse, tokens, ln1_scale, ln1_bias, w3,
        scratch=[
            pltpu.VMEM((2, rows, hidden), BF),
            pltpu.VMEM((LANES, width), F32),
            pltpu.VMEM((rows, width), BF),
        ],
        scalars=1, flops=12 * rows * width * hidden,
    )
    late = reduce_dense(ids, keep, send)
    part1_other = swap(part1, "tensor")
    w_out_t, grad_v_w, small = call(
        early_end_kernel,
        [((piece, hidden), F32), ((piece, hidden), F32), ((piece, LANES), F32)],
        early,
    )
    grad_w_qkv, ln1 = call(
        late_end_kernel,
        [((3, piece, hidden), F32), ((piece, LANES), F32)],
        *late, grad_v_w,
    )
    ln1 = ln1 + swap(ln1, "tensor")
    (grad_tokens,) = call(
        norm1_back_kernel,
        [((rows, width), BF)],
        part1, part1_other, tokens, ln1_scale, ln1_bias, grad_mixed,
    )
    (out_part,) = call(
        functools.partial(gather_out_kernel, sizes),
        [((rows, width), BF)],
        target, out_back.reshape(slots, width),
        flops=2 * slots * rows * width,
    )
    out_other = swap(out_part, "tensor")
    out = (mixed + (out_part.astype(F32) + out_other.astype(F32))).astype(BF)
    return (
        out,
        grad_tokens,
        ln1[:, 0],
        ln1[:, 1],
        grad_w_qkv.transpose(1, 0, 2),
        w_out_t.T,
        small[:, experts],
        small[:, experts + 1],
        small[:, experts + 2],
        small[:, :experts],
        grad_w_in[None],
        biases[:, :inner],
        grad_w_exp_out[None],
        biases[:, inner:],
    )


def solution(mesh):
    rows = P(("dp", "expert"), None)
    shard = P(("dp", "expert"))
    placed = (
        rows,
        P(),
        P(),
        P(None, None, "tensor"),
        P("tensor", None),
        P(),
        P(),
        P(),
        P(),
        P("expert", None, "tensor"),
        P("expert", "tensor"),
        P("expert", "tensor", None),
        P("expert", None),
        rows,
        rows,
    )
    return jax.shard_map(
        per_device,
        mesh=mesh,
        in_specs=placed,
        out_specs=(
            rows,
            rows,
            shard,
            shard,
            P(("dp", "expert"), None, "tensor"),
            P("tensor", ("dp", "expert")),
            shard,
            shard,
            shard,
            rows,
            P("expert", None, "tensor"),
            P("expert", "tensor"),
            P("expert", "tensor", None),
            P("expert", None),
        ),
        check_vma=False,
    )
```

```python
import functools

import jax
import jax.numpy as jnp
from jax import lax
from jax.experimental import pallas as pl
from jax.experimental.pallas import tpu as pltpu
from jax.sharding import PartitionSpec as P


HEAD_DIM = 64
EPSILON = 1e-06
BF = jnp.bfloat16
F32 = jnp.float32
I32 = jnp.int32
LANES = 128
DP, EX, TE = "dp", "expert", "tensor"
SCALING = HEAD_DIM ** (-0.5)

PARAMS = pltpu.CompilerParams(vmem_limit_bytes=60 * 1024 * 1024)


def round_up(value, step):
    return -(-value // step) * step


def layer_norm(values, scale, shift):
    mean_val = jnp.mean(values, axis=-1, keepdims=True)
    centred = values - mean_val
    inv_std = lax.rsqrt(jnp.mean(centred * centred, axis=-1, keepdims=True) + EPSILON)
    x_hat = centred * inv_std
    return (x_hat * scale + shift, x_hat, inv_std)


def norm_back(grad, x_hat, inv_std, scale):
    scaled = grad * scale
    return inv_std * (
        scaled
        - jnp.mean(scaled, axis=-1, keepdims=True)
        - x_hat * jnp.mean(scaled * x_hat, axis=-1, keepdims=True)
    )


def dot32(a, b):
    return jnp.dot(a, b, preferred_element_type=F32)


def dot_nt(a, b):
    return lax.dot_general(a, b, (((1,), (1,)), ((), ())), preferred_element_type=F32)


def dot_tn(a, b):
    return lax.dot_general(a, b, (((0,), (0,)), ((), ())), preferred_element_type=F32)


def iota(shape, dim):
    return lax.broadcasted_iota(I32, shape, dim)


def gelu_both(u):
    c0 = 0.7978845608028654
    square = u * u
    th = jnp.tanh(u * (c0 + (0.044715 * c0) * square))
    half = 0.5 + 0.5 * th
    value = u * half
    slope = half + value * (1.0 - th) * (c0 + (3.0 * 0.044715 * c0) * square)
    return value, slope


def lane_slot(cap_pad):
    lane = iota((cap_pad, LANES), 1)
    slot = iota((cap_pad, LANES), 0)
    match = (lane % cap_pad == slot) & (lane < 2 * cap_pad)
    return match, lane < cap_pad


def with_pad_row(first, column, capacity):
    cap_pad = first.shape[0]
    match, is_high = lane_slot(cap_pad)
    spread = jnp.sum(jnp.where(match, column, 0.0), axis=0, keepdims=True)
    high = spread.astype(BF).astype(F32)
    value = jnp.where(is_high, high, spread - high)
    return jnp.where(iota((cap_pad, LANES), 0) == capacity, value, first)


def from_pad_row(first, capacity):
    cap_pad = first.shape[0]
    match, _ = lane_slot(cap_pad)
    row = jnp.sum(
        jnp.where(iota((cap_pad, LANES), 0) == capacity, first, 0.0), axis=0, keepdims=True
    )
    return jnp.sum(jnp.where(match, row, 0.0), axis=1, keepdims=True)


def row(ref):
    return ref[...].reshape(1, -1)


def route_kernel(sizes, ids_ref, routes_ref, cot_ref, target_ref, buffer_ref):
    rows, experts, capacity, cap_pad = sizes
    slots = experts * cap_pad
    me = ids_ref[0]
    r0, r1 = routes_ref[0:1, :], routes_ref[1:2, :]
    ids = iota((experts, rows), 0)
    hot0 = jnp.where(r0 == ids, 1.0, 0.0)
    hot1 = jnp.where(r1 == ids, 1.0, 0.0)
    before = jnp.where(iota((rows, rows), 0) < iota((rows, rows), 1), 1.0, 0.0).astype(BF)
    earlier0 = dot32(hot0.astype(BF), before)
    earlier1 = dot32(hot1.astype(BF), before) + jnp.sum(hot0, axis=1, keepdims=True)
    slot0 = jnp.sum(earlier0 * hot0, axis=0, keepdims=True).astype(I32)
    slot1 = jnp.sum(earlier1 * hot1, axis=0, keepdims=True).astype(I32)
    a0 = jnp.where(slot0 < capacity, r0 * cap_pad + slot0, slots)
    a1 = jnp.where(slot1 < capacity, r1 * cap_pad + slot1, slots)
    target_ref[...] = jnp.full(target_ref.shape, slots, I32)
    target_ref[0:1, 0:rows] = a0
    target_ref[1:2, 0:rows] = a1
    target_ref[2:3, 0:rows] = jnp.where(slot0 < capacity, (r0 ^ me) * cap_pad + slot0, slots)
    target_ref[3:4, 0:rows] = jnp.where(slot1 < capacity, (r1 ^ me) * cap_pad + slot1, slots)
    ids = iota((slots, rows), 0)
    place = jnp.where((ids == a0) | (ids == a1), 1.0, 0.0).astype(BF)
    buffer_ref[...] = dot32(place, cot_ref[...]).astype(BF)


def attention_kernel(
    tok_ref, scale_ref, shift_ref, w_ref, w_out_ref, part_ref, att_ref, qkv_ref, lse_ref
):
    normed, _, _ = layer_norm(tok_ref[...].astype(F32), row(scale_ref), row(shift_ref))
    normed = normed.astype(BF)
    rows, hidden = att_ref.shape
    for c in range(3):
        qkv_ref[c] = dot32(normed, w_ref[c]).astype(BF)
    low = iota((rows, LANES), 1) < HEAD_DIM
    for pair in range(hidden // LANES):
        cols = slice(pair * LANES, (pair + 1) * LANES)
        q, k, v = qkv_ref[0, :, cols], qkv_ref[1, :, cols], qkv_ref[2, :, cols]
        outs = []
        for part in range(2):
            mine = low if part == 0 else jnp.logical_not(low)
            scores = dot_nt(jnp.where(mine, q, jnp.zeros_like(q)), k) * SCALING
            log_sum = jnp.log(jnp.sum(jnp.exp(scores), axis=1, keepdims=True))
            weights = jnp.exp(scores - log_sum).astype(BF)
            outs.append(dot32(weights, v))
            head = 2 * pair + part
            lse_ref[:, head : head + 1] = log_sum
        att_ref[:, cols] = jnp.where(low, outs[0], outs[1]).astype(BF)
    part_ref[...] = dot32(att_ref[...], w_out_ref[...]).astype(BF)


def middle_kernel(
    sizes,
    tok_ref,
    part_ref,
    part2_ref,
    bias_ref,
    scale_ref,
    shift_ref,
    router_ref,
    routes_ref,
    target_ref,
    mixed_ref,
    probs_ref,
    *block_refs,
):
    rows, experts, capacity, cap_pad = sizes
    slots = experts * cap_pad
    mixed = (
        tok_ref[...].astype(F32)
        + (part_ref[...].astype(F32) + part2_ref[...].astype(F32))
        + row(bias_ref)
    )
    mixed_ref[...] = mixed
    normed, _, _ = layer_norm(mixed, row(scale_ref), row(shift_ref))
    normed = normed.astype(BF)
    exp_logits = jnp.exp(dot_nt(router_ref[...], normed))
    probs = exp_logits / jnp.sum(exp_logits, axis=0, keepdims=True)
    probs_ref[...] = probs
    ids = iota((experts, rows), 0)
    gate0 = jnp.sum(jnp.where(routes_ref[0:1, :] == ids, probs, 0.0), axis=0, keepdims=True)
    gate1 = jnp.sum(jnp.where(routes_ref[1:2, :] == ids, probs, 0.0), axis=0, keepdims=True)
    ids = iota((slots, rows), 0)
    in0 = ids == target_ref[2:3, 0:rows]
    in1 = ids == target_ref[3:4, 0:rows]
    gates = jnp.sum(jnp.where(in0, gate0, jnp.where(in1, gate1, 0.0)), axis=1, keepdims=True)
    picked = dot32(jnp.where(in0 | in1, 1.0, 0.0).astype(BF), normed)
    for k in range(experts):
        span = slice(k * cap_pad, (k + 1) * cap_pad)
        block = picked[span]
        block_refs[k][:, LANES:] = block[:, LANES:].astype(BF)
        block_refs[k][:, :LANES] = with_pad_row(block[:, :LANES], gates[span], capacity).astype(BF)


def expert_kernel(sizes, ids_ref, raw_ref, cot_ref, bias2_ref, w_ref, b_ref, *refs):
    blocks, capacity, cap_pad = sizes
    row_refs = refs[:blocks]
    x_ref, gate_ref, hidden_ref, pre_ref, sent_ref = refs[blocks : blocks + 5]
    back_refs = refs[blocks + 5 : 2 * blocks + 5]
    acc_ref, sg_ref = refs[2 * blocks + 5 :]
    step, last = pl.program_id(0), pl.num_programs(0) - 1

    def place(k):
        return pl.ds(pl.multiple_of((k ^ ids_ref[0]) * cap_pad, cap_pad), cap_pad)

    @pl.when(step == 0)
    def _():
        first = jnp.where(ids_ref[1] == 0, 1.0, 0.0)
        for k in range(blocks):
            span = place(k)
            x_ref[span, :] = row_refs[k][...]
            gate = from_pad_row(row_refs[k][:, :LANES].astype(F32), capacity)
            gate_ref[span, :] = jnp.broadcast_to(gate, (cap_pad, LANES))
            cot = cot_ref[span, :].astype(F32)
            side = jnp.sum(cot * bias2_ref[...], axis=1, keepdims=True)
            sg_ref[span, :] = jnp.broadcast_to(first * side, (cap_pad, LANES))
            sent_ref[span, :] = (gate * cot).astype(BF)

    w = w_ref[...]
    pre_act = dot32(x_ref[...], w) + b_ref[...]
    for k in range(blocks):
        span = slice(k * cap_pad, (k + 1) * cap_pad)
        value, slope = gelu_both(pre_act[span])
        raw = raw_ref[span, :]
        hidden_ref[span, :] = value.astype(BF)
        pre_ref[span, :] = (gate_ref[span, 0:1] * raw * slope).astype(BF)
        side = jnp.sum(value * raw, axis=1, keepdims=True)
        sg_ref[span, :] = sg_ref[span, :] + jnp.broadcast_to(side, (cap_pad, LANES))
    grad = dot_nt(pre_ref[...], w)

    @pl.when(step == 0)
    def _():
        acc_ref[...] = grad

    @pl.when(step > 0)
    def _():
        acc_ref[...] += grad

    @pl.when(step == last)
    def _():
        for k in range(blocks):
            span = place(k)
            back_refs[k][:, LANES:] = acc_ref[span, LANES:].astype(BF)
            first = with_pad_row(acc_ref[span, :LANES], sg_ref[span, 0:1], capacity)
            back_refs[k][:, :LANES] = first.astype(BF)


def combine_kernel(sizes, target_ref, *refs):
    _, experts, capacity, cap_pad = sizes
    block_refs, (pack_ref, x_ref) = refs[:experts], refs[experts:]
    slots = experts * cap_pad
    lanes = target_ref.shape[1]
    body = pack_ref.shape[0] - 16
    gg0 = jnp.zeros((1, lanes), F32)
    gg1 = jnp.zeros((1, lanes), F32)
    for k in range(experts):
        span = slice(k * cap_pad, (k + 1) * cap_pad)
        x_ref[span, :] = block_refs[k][...]
        side = from_pad_row(block_refs[k][:, :LANES].astype(F32), capacity)
        ids = iota((cap_pad, lanes), 0) + k * cap_pad
        gg0 += jnp.sum(jnp.where(ids == target_ref[2:3, :], side, 0.0), axis=0, keepdims=True)
        gg1 += jnp.sum(jnp.where(ids == target_ref[3:4, :], side, 0.0), axis=0, keepdims=True)
    ids = iota((slots, lanes), 0)
    place = jnp.where(
        (ids == target_ref[2:3, :]) | (ids == target_ref[3:4, :]), 1.0, 0.0
    ).astype(BF)
    part = dot_tn(place, x_ref[...])
    pack_ref[0:body, :] = part[0:body].astype(BF)
    pack_ref[body:, :] = jnp.zeros((16, pack_ref.shape[1]), BF)
    line = iota((16, lanes), 0)
    high0, high1 = gg0.astype(BF).astype(F32), gg1.astype(BF).astype(F32)
    tail = jnp.where(line == 0, high0, jnp.where(line == 1, gg0 - high0, 0.0))
    tail = jnp.where(line == 2, high1, jnp.where(line == 3, gg1 - high1, tail))
    pack_ref[body:, 0:lanes] = tail.astype(BF)


def gather_out_kernel(sizes, target_ref, x_ref, out_ref):
    _, experts, _, cap_pad = sizes
    ids = iota((experts * cap_pad, target_ref.shape[1]), 0)
    place = jnp.where(
        (ids == target_ref[0:1, :]) | (ids == target_ref[1:2, :]), 1.0, 0.0
    ).astype(BF)
    out_ref[...] = dot_tn(place, x_ref[...])[0 : out_ref.shape[0]].astype(BF)


def halves(ids_ref, width):
    half = width // 2
    return (
        pl.ds(pl.multiple_of(ids_ref[2] * half, LANES), half),
        pl.ds(pl.multiple_of((1 - ids_ref[2]) * half, LANES), half),
    )


def norm2_back_kernel(
    sizes,
    ids_ref,
    pack_ref,
    pack2_ref,
    mixed_ref,
    probs_ref,
    routes_ref,
    router_ref,
    cot_ref,
    scale_ref,
    shift_ref,
    att_ref,
    w_out_ref,
    qkv_ref,
    lse_ref,
    tok_ref,
    scale1_ref,
    shift1_ref,
    grad_ref,
    grad_att_ref,
    grad_v_ref,
    keep_ref,
    send_ref,
    small_ref,
    left_ref,
):
    rows, experts, _, _ = sizes
    width = tok_ref.shape[1]
    hidden = att_ref.shape[1]
    body = pack_ref.shape[0] - 16
    tail = pack_ref[body:, 0:rows].astype(F32) + pack2_ref[body:, 0:rows].astype(F32)
    gg0 = tail[0:1] + tail[1:2]
    gg1 = tail[2:3] + tail[3:4]
    ids = iota((experts, rows), 0)
    grad_probs = jnp.where(routes_ref[0:1, :] == ids, gg0, 0.0) + jnp.where(
        routes_ref[1:2, :] == ids, gg1, 0.0
    )
    probs = probs_ref[...]
    grad_logits = probs * (grad_probs - jnp.sum(probs * grad_probs, axis=0, keepdims=True))
    grad_logits = grad_logits.astype(BF)
    grad_normed = (
        pack_ref[0:rows, :].astype(F32)
        + pack2_ref[0:rows, :].astype(F32)
        + dot_tn(grad_logits, router_ref[...])
    )
    normed, x_hat, inv_std = layer_norm(mixed_ref[...], row(scale_ref), row(shift_ref))
    grad_mixed = cot_ref[...].astype(F32) + norm_back(grad_normed, x_hat, inv_std, row(scale_ref))
    grad_ref[...] = grad_mixed
    left_ref[...] = grad_mixed.astype(BF)
    sides = tuple(zip((keep_ref, send_ref), halves(ids_ref, width)))
    for ref, cols in sides:
        ref[:, 0:hidden] = dot_tn(left_ref[:, cols], att_ref[...]).astype(BF)
    small_ref[...] = jnp.zeros_like(small_ref)
    small_ref[0:experts, :] = dot32(grad_logits, normed.astype(BF))
    small_ref[experts : experts + 1, :] = jnp.sum(grad_mixed, axis=0, keepdims=True)
    small_ref[experts + 1 : experts + 2, :] = jnp.sum(grad_normed * x_hat, axis=0, keepdims=True)
    small_ref[experts + 2 : experts + 3, :] = jnp.sum(grad_normed, axis=0, keepdims=True)
    for ref, cols in sides:
        ref[:, 2 * hidden :] = small_ref[:, cols].T.astype(BF)
    grad_att_ref[...] = dot_nt(left_ref[...], w_out_ref[...]).astype(BF)
    low = iota((rows, LANES), 1) < HEAD_DIM
    for pair in range(hidden // LANES):
        cols = slice(pair * LANES, (pair + 1) * LANES)
        q, k = qkv_ref[0, :, cols], qkv_ref[1, :, cols]
        g = grad_att_ref[:, cols]
        outs = []
        for part in range(2):
            mine = low if part == 0 else jnp.logical_not(low)
            head = 2 * pair + part
            scores = dot_nt(jnp.where(mine, q, jnp.zeros_like(q)), k) * SCALING
            weights = jnp.exp(scores - lse_ref[:, head : head + 1])
            outs.append(dot_tn(weights.astype(BF), g))
        grad_v_ref[:, cols] = jnp.where(low, outs[0], outs[1]).astype(BF)
    normed1, _, _ = layer_norm(tok_ref[...].astype(F32), row(scale1_ref), row(shift1_ref))
    left_ref[...] = normed1.astype(BF)
    for ref, cols in sides:
        ref[:, hidden : 2 * hidden] = dot_tn(left_ref[:, cols], grad_v_ref[...]).astype(BF)


def attention_back_kernel(
    ids_ref,
    grad_att_ref,
    grad_v_ref,
    qkv_ref,
    lse_ref,
    tok_ref,
    scale_ref,
    shift_ref,
    w_ref,
    part_ref,
    keep_ref,
    send_ref,
    gqk_ref,
    small_ref,
    left_ref,
):
    rows, width = tok_ref.shape
    hidden = grad_att_ref.shape[1]
    low = iota((rows, LANES), 1) < HEAD_DIM
    for pair in range(hidden // LANES):
        cols = slice(pair * LANES, (pair + 1) * LANES)
        q, k, v = qkv_ref[0, :, cols], qkv_ref[1, :, cols], qkv_ref[2, :, cols]
        g = grad_att_ref[:, cols]
        outs = []
        for part in range(2):
            mine = low if part == 0 else jnp.logical_not(low)
            head = 2 * pair + part
            scores = dot_nt(jnp.where(mine, q, jnp.zeros_like(q)), k) * SCALING
            weights = jnp.exp(scores - lse_ref[:, head : head + 1])
            grad_w = dot_nt(jnp.where(mine, g, jnp.zeros_like(g)), v)
            delta = jnp.sum(weights * grad_w, axis=1, keepdims=True)
            grad_s = (weights * (grad_w - delta) * SCALING).astype(BF)
            outs.append((dot32(grad_s, k), dot_tn(grad_s, q)))
        for c in range(2):
            gqk_ref[c, :, cols] = jnp.where(low, outs[0][c], outs[1][c]).astype(BF)
    part = dot_nt(gqk_ref[0], w_ref[0]) + dot_nt(gqk_ref[1], w_ref[1]) + dot_nt(grad_v_ref[...], w_ref[2])
    part_ref[...] = part.astype(BF)
    normed, x_hat, _ = layer_norm(tok_ref[...].astype(F32), row(scale_ref), row(shift_ref))
    left_ref[...] = normed.astype(BF)
    small_ref[...] = jnp.zeros_like(small_ref)
    small_ref[0:1, :] = jnp.sum(part * x_hat, axis=0, keepdims=True)
    small_ref[1:2, :] = jnp.sum(part, axis=0, keepdims=True)
    for ref, cols in zip((keep_ref, send_ref), halves(ids_ref, width)):
        for c in range(2):
            ref[:, c * hidden : (c + 1) * hidden] = dot_tn(left_ref[:, cols], gqk_ref[c]).astype(BF)
        ref[:, 2 * hidden :] = small_ref[:, cols].T.astype(BF)


def norm1_back_kernel(part_ref, part2_ref, tok_ref, scale_ref, shift_ref, grad_ref, out_ref):
    grad = part_ref[...].astype(F32) + part2_ref[...].astype(F32)
    _, x_hat, inv_std = layer_norm(tok_ref[...].astype(F32), row(scale_ref), row(shift_ref))
    out_ref[...] = (grad_ref[...] + norm_back(grad, x_hat, inv_std, row(scale_ref))).astype(BF)


def early_end_kernel(part_ref, w_out_ref, v_ref, router_ref, b_ref, scale_ref, shift_ref, turn_ref):
    piece, hidden = v_ref.shape
    experts = router_ref.shape[0]
    total = part_ref[0].astype(F32)
    for k in range(1, part_ref.shape[0]):
        total = total + part_ref[k].astype(F32)
    w_out_ref[...] = total[:, :hidden]
    v_ref[...] = total[:, hidden : 2 * hidden]
    turn_ref[...] = jnp.zeros_like(turn_ref)
    turn_ref[0:piece, :] = total[:, 2 * hidden :]
    turned = turn_ref[...].T
    router_ref[...] = turned[0:experts, 0:piece]
    b_ref[...] = turned[experts : experts + 1, 0:piece]
    scale_ref[...] = turned[experts + 1 : experts + 2, 0:piece]
    shift_ref[...] = turned[experts + 2 : experts + 3, 0:piece]


def late_end_kernel(kept_ref, got_ref, v_ref, qkv_ref, ln1_ref, turn_ref):
    piece, hidden = v_ref.shape
    total = kept_ref[0].astype(F32) + got_ref[0].astype(F32)
    turn_ref[...] = jnp.zeros_like(turn_ref)
    turn_ref[0:piece, :] = total[:, 2 * hidden :]
    ln1_ref[...] = turn_ref[...].T[0:8]
    qkv_ref[0] = total[:, :hidden]
    qkv_ref[1] = total[:, hidden : 2 * hidden]
    qkv_ref[2] = v_ref[...]


def weight_grad_kernel(ids_ref, a_ref, a2_ref, b_ref, b2_ref, out_ref, sum_ref):
    @pl.when(pl.program_id(0) == 0)
    def _():
        own = jnp.sum(b_ref[...].astype(F32), axis=0, keepdims=True)
        sum_ref[...] = own + jnp.sum(b2_ref[...].astype(F32), axis=0, keepdims=True)

    @pl.when(ids_ref[2] == 0)
    def _():
        out_ref[...] = dot_tn(a_ref[...], b_ref[...]) + dot_tn(a2_ref[...], b2_ref[...])

    @pl.when(ids_ref[2] == 1)
    def _():
        out_ref[...] = dot_tn(a2_ref[...], b2_ref[...]) + dot_tn(a_ref[...], b_ref[...])


def weight_grad(ids, a, a2, b, b2):
    slots, rows = a.shape
    cols = b.shape[1]
    tile = 512 if rows % 512 == 0 and rows > cols else 256
    left = pl.BlockSpec((slots, tile), lambda i: (0, i))
    right = pl.BlockSpec((slots, cols), lambda i: (0, 0))
    return pl.pallas_call(
        weight_grad_kernel,
        grid=(rows // tile,),
        out_shape=[
            jax.ShapeDtypeStruct((rows, cols), F32),
            jax.ShapeDtypeStruct((1, cols), F32),
        ],
        in_specs=[pl.BlockSpec(memory_space=pltpu.SMEM), left, left, right, right],
        out_specs=[
            pl.BlockSpec((tile, cols), lambda i: (i, 0)),
            pl.BlockSpec((1, cols), lambda i: (0, 0)),
        ],
        compiler_params=PARAMS,
        cost_estimate=pl.CostEstimate(
            flops=4 * slots * rows * cols, bytes_accessed=9_000_000, transcendentals=0
        ),
    )(ids, a, a2, b, b2)


def call(kernel, outs, *args, scratch=(), scalars=0, flops=0):
    specs = [
        pl.BlockSpec(memory_space=pltpu.SMEM if i < scalars else pltpu.VMEM)
        for i in range(len(args))
    ]
    moved = sum(a.size * a.dtype.itemsize for a in args)
    return pl.pallas_call(
        kernel,
        out_shape=tuple(jax.ShapeDtypeStruct(s, d) for s, d in outs),
        in_specs=specs,
        out_specs=tuple(pl.BlockSpec(memory_space=pltpu.VMEM) for _ in outs),
        scratch_shapes=list(scratch),
        compiler_params=PARAMS,
        cost_estimate=pl.CostEstimate(flops=flops, bytes_accessed=moved, transcendentals=0),
    )(*args)


def swap(x, axis):
    return lax.ppermute(x, axis, [(0, 1), (1, 0)])


def xor_exchange(blocks, count, order):
    outs = {}
    for k in order:
        outs[k] = lax.ppermute(blocks[k], EX, [(i, i ^ k) for i in range(count)])
    return outs


def all_to_all(x):
    return lax.all_to_all(x, EX, split_axis=0, concat_axis=0, tiled=True)


def reduce_dense(ids, keep, send):
    count = lax.axis_size(EX)
    piece = keep.shape[0] // count
    cols = keep.shape[1]
    got = swap(send, DP).reshape(count, piece, cols)
    keep = keep.reshape(count, piece, cols)
    bit, left = 0, count
    while left > 1:
        left //= 2
        mine = (ids[0] >> bit) & 1
        pair = (left, 2, piece, cols)

        def half_sum(which):
            return (
                lax.dynamic_index_in_dim(keep.reshape(pair), which, 1, keepdims=False).astype(F32)
                + lax.dynamic_index_in_dim(got.reshape(pair), which, 1, keepdims=False).astype(F32)
            ).astype(BF)

        send, keep = half_sum(1 - mine), half_sum(mine)
        got = lax.ppermute(send, EX, [(i, i ^ (1 << bit)) for i in range(count)])
        bit += 1
    return keep, got


def per_device(
    tokens,
    ln1_scale,
    ln1_bias,
    w_qkv,
    w_out,
    b_out,
    ln2_scale,
    ln2_bias,
    w_router,
    w_in,
    b_in,
    w_exp_out,
    b_exp_out,
    routes,
    cotangent,
):
    rows, width = tokens.shape
    experts = w_router.shape[1]
    count = lax.axis_size(EX)
    ids = jnp.stack(
        [lax.axis_index(EX), lax.axis_index(TE), lax.axis_index(DP)]
    ).astype(I32)
    capacity = (5 * rows + 2 * experts - 1) // (2 * experts)
    cap_pad = round_up(capacity + 1, 16)
    slots = experts * cap_pad
    hidden = w_qkv.shape[2]
    inner = w_in.shape[2]
    lanes = round_up(rows, LANES)
    half = width // 2
    sizes = (rows, experts, capacity, cap_pad)
    w_in, w_exp_out = w_in[0], w_exp_out[0]
    w3 = w_qkv.transpose(1, 0, 2)
    router_t = w_router.T
    routes_t = routes.T

    target, cot_buffer = call(
        functools.partial(route_kernel, sizes),
        [((4, lanes), I32), ((slots, width), BF)],
        ids, routes_t, cotangent,
        scalars=1, flops=2 * slots * rows * width,
    )
    cot_rows = all_to_all(cot_buffer.reshape(experts, cap_pad, width))
    part, attended, qkv, lse = call(
        attention_kernel,
        [((rows, width), BF), ((rows, hidden), BF), ((3, rows, hidden), BF), ((rows, LANES), F32)],
        tokens, ln1_scale, ln1_bias, w3, w_out,
        flops=8 * rows * width * hidden,
    )
    part_other = swap(part, TE)
    mixed, probs, *blocks = call(
        functools.partial(middle_kernel, sizes),
        [((rows, width), F32), ((experts, rows), F32)] + [((cap_pad, width), BF)] * experts,
        tokens, part, part_other, b_out, ln2_scale, ln2_bias, router_t, routes_t, target,
        flops=2 * slots * rows * width,
    )
    order = tuple(range(experts - 1, 0, -1))
    received = xor_exchange(blocks, count, order)
    received[0] = blocks[0]

    tile = 512
    whole = lambda shape: pl.BlockSpec(shape, lambda f: (0,) * len(shape))
    wide = pl.BlockSpec((slots, tile), lambda f: (0, f))
    cot_rows = cot_rows.reshape(slots, width)
    raw = dot_nt(cot_rows, w_exp_out)
    outs = pl.pallas_call(
        functools.partial(expert_kernel, (experts, capacity, cap_pad)),
        grid=(inner // tile,),
        out_shape=[
            jax.ShapeDtypeStruct((slots, width), BF),
            jax.ShapeDtypeStruct((slots, LANES), F32),
            jax.ShapeDtypeStruct((slots, inner), BF),
            jax.ShapeDtypeStruct((slots, inner), BF),
            jax.ShapeDtypeStruct((slots, width), BF),
        ]
        + [jax.ShapeDtypeStruct((cap_pad, width), BF)] * experts,
        in_specs=[
            pl.BlockSpec(memory_space=pltpu.SMEM),
            wide,
            whole((slots, width)),
            whole((1, width)),
            pl.BlockSpec((width, tile), lambda f: (0, f)),
            pl.BlockSpec((1, tile), lambda f: (0, f)),
        ]
        + [whole((cap_pad, width))] * experts,
        out_specs=[whole((slots, width)), whole((slots, LANES)), wide, wide, whole((slots, width))]
        + [whole((cap_pad, width))] * experts,
        scratch_shapes=[pltpu.VMEM((slots, width), F32), pltpu.VMEM((slots, LANES), F32)],
        compiler_params=PARAMS,
        cost_estimate=pl.CostEstimate(
            flops=4 * slots * width * inner, bytes_accessed=12_000_000, transcendentals=0
        ),
    )(ids, raw, cot_rows, b_exp_out, w_in, b_in, *[received[k] for k in range(experts)])
    x_rows, gate, hidden_act, grad_pre, grad_sent = outs[:5]
    back = xor_exchange(outs[5:], count, order)
    back[0] = outs[5]
    own_bias = jnp.where(lax.axis_index(TE) == 0, b_exp_out, 0.0)
    out_rows = gate[:, :1] * (dot32(hidden_act, w_exp_out) + own_bias)
    out_rows = out_rows.astype(BF).reshape(experts, cap_pad, width)
    x_other = swap(x_rows, DP)
    pre_other = swap(grad_pre, DP)
    hidden_other = swap(hidden_act, DP)
    sent_other = swap(grad_sent, DP)
    grad_w_in, grad_b_in = weight_grad(ids, x_rows, x_other, grad_pre, pre_other)
    grad_w_exp_out, grad_b_exp_out = weight_grad(
        ids, hidden_act, hidden_other, grad_sent, sent_other
    )
    body = round_up(rows, 16)
    (pack,) = call(
        functools.partial(combine_kernel, sizes),
        [((body + 16, width), BF)],
        target, *[back[k] for k in range(experts)],
        scratch=[pltpu.VMEM((slots, width), BF)],
        flops=2 * slots * rows * width,
    )
    pack_other = swap(pack, TE)
    out_rows, pack = lax.optimization_barrier((out_rows, pack))
    out_back = all_to_all(out_rows)
    grad_mixed, grad_att, grad_v, keep, send = call(
        functools.partial(norm2_back_kernel, sizes),
        [
            ((rows, width), F32),
            ((rows, hidden), BF),
            ((rows, hidden), BF),
            ((half, 2 * hidden + LANES), BF),
            ((half, 2 * hidden + LANES), BF),
        ],
        ids, pack, pack_other, mixed, probs, routes_t, router_t, cotangent, ln2_scale,
        ln2_bias, attended, w_out, qkv, lse, tokens, ln1_scale, ln1_bias,
        scratch=[pltpu.VMEM((LANES, width), F32), pltpu.VMEM((rows, width), BF)],
        scalars=1, flops=8 * rows * width * hidden,
    )
    piece = half // count
    got = swap(send, DP)
    early = (keep.astype(F32) + got.astype(F32)).astype(BF)
    early = all_to_all(early.reshape(count, piece, -1))
    part1, keep, send = call(
        attention_back_kernel,
        [((rows, width), BF), ((half, 2 * hidden + LANES), BF), ((half, 2 * hidden + LANES), BF)],
        ids, grad_att, grad_v, qkv, lse, tokens, ln1_scale, ln1_bias, w3,
        scratch=[
            pltpu.VMEM((2, rows, hidden), BF),
            pltpu.VMEM((LANES, width), F32),
            pltpu.VMEM((rows, width), BF),
        ],
        scalars=1, flops=12 * rows * width * hidden,
    )
    late = reduce_dense(ids, keep, send)
    part1_other = swap(part1, TE)
    w_out_t, grad_v_w, router_rows, b_row, scale_row, shift_row = call(
        early_end_kernel,
        [((piece, hidden), F32), ((piece, hidden), F32), ((experts, piece), F32)]
        + [((1, piece), F32)] * 3,
        early,
        scratch=[pltpu.VMEM((LANES, LANES), F32)],
    )
    grad_w_qkv, ln1 = call(
        late_end_kernel,
        [((3, piece, hidden), F32), ((8, LANES), F32)],
        *late, grad_v_w,
        scratch=[pltpu.VMEM((LANES, LANES), F32)],
    )
    ln1 = ln1 + swap(ln1, TE)
    (grad_tokens,) = call(
        norm1_back_kernel,
        [((rows, width), BF)],
        part1, part1_other, tokens, ln1_scale, ln1_bias, grad_mixed,
    )
    (out_part,) = call(
        functools.partial(gather_out_kernel, sizes),
        [((rows, width), BF)],
        target, out_back.reshape(slots, width),
        flops=2 * slots * rows * width,
    )
    out_other = swap(out_part, TE)
    out = (mixed + (out_part.astype(F32) + out_other.astype(F32))).astype(BF)
    return (
        out,
        grad_tokens,
        ln1[0, :piece],
        ln1[1, :piece],
        grad_w_qkv.transpose(1, 0, 2),
        w_out_t.T,
        b_row.reshape(piece),
        scale_row.reshape(piece),
        shift_row.reshape(piece),
        router_rows.T,
        grad_w_in[None],
        grad_b_in,
        grad_w_exp_out[None],
        grad_b_exp_out,
    )


def solution(mesh):
    rows = P((DP, EX), None)
    shard = P((DP, EX))
    placed = (
        rows,
        P(),
        P(),
        P(None, None, TE),
        P(TE, None),
        P(),
        P(),
        P(),
        P(),
        P(EX, None, TE),
        P(EX, TE),
        P(EX, TE, None),
        P(EX, None),
        rows,
        rows,
    )
    return jax.shard_map(
        per_device,
        mesh=mesh,
        in_specs=placed,
        out_specs=(
            rows,
            rows,
            shard,
            shard,
            P((DP, EX), None, TE),
            P(TE, (DP, EX)),
            shard,
            shard,
            shard,
            rows,
            P(EX, None, TE),
            P(EX, TE),
            P(EX, TE, None),
            P(EX, None),
        ),
        check_vma=False,
    )
```
